768 devices in a mesh: gx: 8 (over y), gy: 16 (over z_lo, x), gz: 6 (over z_hi, core).
Axes of the slice: x: 4, y: 8, z: 12 (z_hi: 3, z_lo: 4; z = z_hi * 4 + z_lo), core: 2. Of those that a mesh axis runs over, the one named last changes fastest.
Arguments:
- positions: float32 [16, 32, 6, 192], P('gx', 'gy', 'gz'), may hold values from 0 to 1
- species: int32 [16, 32, 6, 64], P('gx', 'gy', 'gz'), may hold values from 0 to 88
- counts: int32 [16, 32, 6], P('gx', 'gy', 'gz'), may hold values from 1 to 64, as said below
- embed: bfloat16 [89, 128], replicated, may hold values from -6 to 6
- filters: bfloat16 [128, 512], replicated, may hold values from -0.5 to 0.5
- w_up: bfloat16 [128, 128], replicated, may hold values from -0.5 to 0.5
- w_energy: float32 [128], replicated, may hold values from -0.5 to 0.5
Outputs:
- energies: float32 [16, 32, 6, 64], P('gx', 'gy', 'gz')
- forces: float32 [16, 32, 6, 192], P('gx', 'gy', 'gz')
The draws below stay inside these ranges and needn't reach their ends.
Inputs may be any that keep to these rules, and one draw needn't show every extreme that they name: `counts`: at most 64 atoms a cell; some cell holds exactly 64 and some exactly 1.
All inputs are finite; a program needn't handle non-finite values.
Results may differ from the reference program's by a relative error of at most 0.0038.
Values may be sent and summed in bfloat16 or wider, within the bound.
A program may use at most 32 MiB of HBM per device.

```python
import jax
import jax.numpy as jnp
from jax import lax

CH = 128
RAD = 4
NSPEC = 89
SLOTS = 64
BX = 16
BY = 32
BZ = 6


def draw_counts(key, part):
    counts = jax.random.randint(key, (BX, BY, BZ), 1, SLOTS + 1)
    counts = counts.at[0, 0, 0].set(SLOTS)
    counts = counts.at[0, 0, 1].set(1)
    return counts.astype(jnp.int32)


def plant(values, rng, least, largest):
    spot = [jax.random.randint(jax.random.fold_in(rng, axis), (), 0, length) for axis, length in enumerate(values.shape)]
    longest = values.shape.index(max(values.shape))
    neighbour = spot[:longest] + [(spot[longest] + 1) % values.shape[longest]] + spot[longest + 1:]
    return values.at[tuple(spot)].set(least).at[tuple(neighbour)].set(largest)


def shard_levels(rng, dims, cuts, least, top_value):
    gain, own = 1.0, jax.random.fold_in(rng, 6)
    for position, shards_of in cuts:
        draws = jnp.exp(jax.random.uniform(jax.random.fold_in(own, position), (shards_of,), jnp.float32, least / len(cuts), top_value / len(cuts)))
        gain = gain * jnp.repeat(draws, dims[position] // shards_of).reshape([-1 if axis == position else 1 for axis in range(len(dims))])
    return gain


def gaussian(key, shape, scale, bound, kind=jnp.bfloat16):
    values = scale * jax.random.normal(key, shape, jnp.float32)
    return jnp.clip(values, min=-bound, max=bound).astype(kind)


def setup_inputs(seed: int = 0) -> dict:
    key_list = jax.random.split(jax.random.key(seed), 8)
    positions = jnp.clip(1.0 * jax.random.uniform(key_list[0], (BX, BY, BZ, 3 * SLOTS), jnp.float32) ** shard_levels(key_list[0], (BX, BY, BZ, 3 * SLOTS), ((0, 8), (1, 16), (2, 6)), -0.2, 0.2), 0.0, 1.0)
    species = plant(jax.random.randint(key_list[1], (BX, BY, BZ, SLOTS), 0, NSPEC), jax.random.fold_in(key_list[1], 1), 0, NSPEC - 1).astype(jnp.int32)
    counts = draw_counts(jax.random.fold_in(key_list[7], 71), 0)
    embed = gaussian(key_list[3], (NSPEC, CH), 1.0, 6.0)
    filters = gaussian(key_list[4], (CH, RAD * CH), CH ** -0.5, 0.5)
    w_up = gaussian(key_list[5], (CH, CH), CH ** -0.5, 0.5)
    w_energy = gaussian(key_list[6], (CH,), CH ** -0.5, 0.5, jnp.float32)
    return dict(positions=positions, species=species, counts=counts, embed=embed, filters=filters, w_up=w_up, w_energy=w_energy)


MSG_SCALE = 0.1


def rounded(values):
    return lax.optimization_barrier(values.astype(jnp.bfloat16)).astype(jnp.float32)


def radial(dist_sq, radial_count):
    decay_rates = 0.5 * 3.0 ** jnp.arange(radial_count).astype(jnp.float32)
    falloff = jnp.maximum(1.0 - dist_sq, 0.0)[..., None]
    decaying = jnp.exp(-decay_rates * dist_sq[..., None])
    return decaying * falloff * falloff, -decaying * (decay_rates * falloff * falloff + 2.0 * falloff)


def geometry(anchor_pos, target_pos, offset):
    slot_count = anchor_pos.shape[-1] // 3
    leading = anchor_pos.shape[:-1]
    anchor = anchor_pos.reshape(leading + (3, slot_count))
    target = target_pos.reshape(leading + (3, slot_count))
    shift_vec = jnp.array(offset, jnp.float32).reshape((3, 1, 1))
    displace = target[..., :, None, :] - anchor[..., :, :, None] + shift_vec
    return displace, jnp.sum(displace * displace, axis=-3)


def window(padded, offset, cell_shape):
    return padded[1 + offset[0]:1 + offset[0] + cell_shape[0], 1 + offset[1]:1 + offset[1] + cell_shape[1], 1 + offset[2]:1 + offset[2] + cell_shape[2]]


def all_offsets():
    return [(first, second, third) for first in (-1, 0, 1) for second in (-1, 0, 1) for third in (-1, 0, 1)]


def slab_messages(pos_slab, feat_slab, cell_shape, slot_count, radial_count, feature_width):
    anchor_pos = window(pos_slab, (0, 0, 0), cell_shape)
    diagonal = jnp.eye(slot_count, dtype=jnp.float32)[..., None]
    message = jnp.zeros(cell_shape + (slot_count, feature_width), jnp.float32)
    for offset in all_offsets():
        target_pos = window(pos_slab, offset, cell_shape)
        target_feat = window(feat_slab, offset, cell_shape).reshape(cell_shape + (slot_count * radial_count, feature_width))
        displace, dist_sq = geometry(anchor_pos, target_pos, offset)
        radial_vals = radial(dist_sq, radial_count)[0]
        if offset == (0, 0, 0):
            radial_vals = radial_vals * (1.0 - diagonal)
        weights = rounded(radial_vals.reshape(cell_shape + (slot_count, slot_count * radial_count)))
        message = message + jnp.einsum("abcip,abcpd->abcid", weights, target_feat.astype(jnp.float32))
    return MSG_SCALE * message


def slab_forces(pos_slab, feat_slab, adj_slab, cell_shape, slot_count, radial_count, feature_width):
    anchor_pos = window(pos_slab, (0, 0, 0), cell_shape)
    anchor_adj = window(adj_slab, (0, 0, 0), cell_shape).astype(jnp.float32)
    anchor_feat = window(feat_slab, (0, 0, 0), cell_shape).reshape(cell_shape + (slot_count * radial_count, feature_width)).astype(jnp.float32)
    forces = jnp.zeros(cell_shape + (3, slot_count), jnp.float32)
    for offset in all_offsets():
        target_pos = window(pos_slab, offset, cell_shape)
        target_feat = window(feat_slab, offset, cell_shape).reshape(cell_shape + (slot_count * radial_count, feature_width)).astype(jnp.float32)
        target_adj = window(adj_slab, offset, cell_shape).astype(jnp.float32)
        displace, dist_sq = geometry(anchor_pos, target_pos, offset)
        radial_slope = radial(dist_sq, radial_count)[1]
        outward = jnp.einsum("abcid,abcpd->abcip", anchor_adj, target_feat).reshape(cell_shape + (slot_count, slot_count, radial_count))
        inward = jnp.einsum("abcjd,abcpd->abcjp", target_adj, anchor_feat).reshape(cell_shape + (slot_count, slot_count, radial_count))
        inward = jnp.swapaxes(inward, -3, -2)
        pair_weight = MSG_SCALE * jnp.sum(radial_slope * (outward + inward), axis=-1)
        forces = forces + 2.0 * jnp.sum(displace * pair_weight[..., None, :, :], axis=-1)
    return forces


def periodic(values):
    return jnp.pad(values, ((1, 1), (1, 1), (1, 1)) + ((0, 0),) * (values.ndim - 3), mode="wrap")


def reference(positions, species, counts, embed, filters, w_up, w_energy):
    slot_count = species.shape[-1]
    feature_width = embed.shape[1]
    radial_count = filters.shape[1] // feature_width
    occupied = (jnp.arange(slot_count, dtype=jnp.int32) < counts[..., None]).astype(jnp.float32)
    embedded = (embed[species].astype(jnp.float32) * occupied[..., None]).astype(jnp.bfloat16)

    def project_plane(plane):
        return jnp.einsum("bcsd,de->bcse", plane.astype(jnp.float32), filters.astype(jnp.float32)).astype(jnp.bfloat16)

    projected = lax.map(project_plane, embedded)
    pos_pad = periodic(positions)
    feat_pad = periodic(projected)
    plane_shape = (1,) + positions.shape[1:3]

    def messages_at(row):
        pos_slab = lax.dynamic_slice_in_dim(pos_pad, row, 3, 0)
        feat_slab = lax.dynamic_slice_in_dim(feat_pad, row, 3, 0)
        return slab_messages(pos_slab, feat_slab, plane_shape, slot_count, radial_count, feature_width)[0]

    rows = jnp.arange(positions.shape[0], dtype=jnp.int32)
    message = lax.map(messages_at, rows)
    sigmoid_msg = jax.nn.sigmoid(message)
    activated = rounded(message * sigmoid_msg)
    hidden = embedded.astype(jnp.float32) + jnp.einsum("xyzsd,de->xyzse", activated, w_up.astype(jnp.float32))
    energies = occupied * jnp.sum(hidden * w_energy, axis=-1)
    readout = jnp.sum(w_up.astype(jnp.float32) * w_energy[None, :], axis=1)
    adjoint = (occupied[..., None] * sigmoid_msg * (1.0 + message * (1.0 - sigmoid_msg)) * readout).astype(jnp.bfloat16)
    adj_pad = periodic(adjoint)

    def forces_at(row):
        pos_slab = lax.dynamic_slice_in_dim(pos_pad, row, 3, 0)
        feat_slab = lax.dynamic_slice_in_dim(feat_pad, row, 3, 0)
        adj_slab = lax.dynamic_slice_in_dim(adj_pad, row, 3, 0)
        return slab_forces(pos_slab, feat_slab, adj_slab, plane_shape, slot_count, radial_count, feature_width)[0]

    forces = lax.map(forces_at, rows)
    forces = (forces * occupied[..., None, :]).reshape(positions.shape)
    return energies, forces
```

```python
import functools

import jax
import jax.numpy as jnp
from jax import lax
from jax.experimental import pallas as pl
from jax.experimental.pallas import tpu as pltpu
from jax.sharding import PartitionSpec as P

MESH = pl.DeviceIdType.MESH
F32 = jnp.float32
BF16 = jnp.bfloat16

SLOTS = 64
CH = 128
RAD = 4
SPEC = 128
MSG_SCALE = 0.1

CENTRE, NEAR, FAR = 0, 1, 2
NT = (((1,), (1,)), ((), ()))
NN = (((1,), (0,)), ((), ()))

DIRS = [
    (role, dx, dy)
    for role in (FAR, CENTRE, NEAR)
    for dx, dy in ((1, 1), (1, -1), (-1, 1), (-1, -1), (0, 1), (0, -1), (1, 0), (-1, 0), (0, 0))
    if (role, dx, dy) != (CENTRE, 0, 0)
]


def dot(a, b, dims=NN, precision=None):
    return lax.dot_general(a, b, dims, precision=precision, preferred_element_type=F32)


def pieces(values, count):
    out = []
    for _ in range(count):
        out.append(values.astype(BF16))
        values = values - out[-1].astype(F32)
    return out


def own_part(step):
    return {1: (1, 2), -1: (0, 1), 0: (0, 2)}[step]


def halo_part(step):
    return {1: (3, 4), -1: (0, 1), 0: (1, 3)}[step]


def near_tiles(c):
    ix, iy = c // 2, c % 2
    return [(ix + a) * 4 + iy + b for a in range(3) for b in range(3)]


def far_tiles(c):
    iy = c % 2
    return [16 + a * 4 + iy + b for a in range(2) for b in range(3)]


def kernel(
    sizes,
    cnt_ref,
    pos_ref,
    spec_ref,
    embed_ref,
    filt_ref,
    wup_ref,
    we_ref,
    en_ref,
    fo_ref,
    pad,
    rec,
    back,
    xz,
    ys,
    hot,
    anchor,
    table,
    rows,
    emb,
    wbuf,
    sbuf,
    abuf,
    act,
    racc,
    dacc,
    send1,
    recv1,
    send2,
    recv2,
):
    nx, ny, nz = sizes
    gx, gy, gz = (lax.axis_index(name) for name in ("gx", "gy", "gz"))
    odd = lax.rem(gz, 2)
    roles = (gz, gz + 1 - 2 * odd, lax.rem(gz + nz - 1 + 2 * odd, nz))

    def device(role, dx, dy):
        return (lax.rem(gx + nx + dx, nx), lax.rem(gy + ny + dy, ny), roles[role])

    barrier = pltpu.get_barrier_semaphore()
    for d in DIRS:
        pl.semaphore_signal(barrier, inc=1, device_id=device(*d), device_id_type=MESH)

    slot_lane = lax.broadcasted_iota(jnp.int32, (1, SLOTS), 1)
    for c in range(4):
        marked = jnp.where(slot_lane < cnt_ref[c], spec_ref[c : c + 1, :], -1).astype(F32)
        pad[CENTRE, 1 + c // 2, 1 + c % 2, 0:1, :] = pos_ref[c : c + 1, 0:128]
        pad[CENTRE, 1 + c // 2, 1 + c % 2, 1:2, :] = jnp.concatenate(
            [pos_ref[c : c + 1, 128:192], marked], axis=1
        )
    eye = lax.broadcasted_iota(jnp.int32, (SLOTS, SLOTS), 0) == lax.broadcasted_iota(
        jnp.int32, (SLOTS, SLOTS), 1
    )
    for c in range(4):
        for q in range(3):
            row = jnp.broadcast_to(pos_ref[c : c + 1, q * SLOTS : (q + 1) * SLOTS], (SLOTS, SLOTS))
            column = jnp.sum(jnp.where(eye, row, 0.0), axis=1, keepdims=True)
            shift = (1.0 + c // 2, 1.0 + c % 2, 0.0)[q]
            anchor[c, q] = jnp.broadcast_to(column + shift, (SLOTS, 128))
    emb[...] = jnp.zeros_like(emb)
    emb[0 : embed_ref.shape[0], :] = embed_ref[...].astype(F32)
    embedding = emb[...].astype(BF16)
    for k in range(RAD):
        table[k * SPEC : (k + 1) * SPEC, :] = dot(
            embedding, filt_ref[:, k * CH : (k + 1) * CH]
        ).astype(BF16)
    energy_rows = jnp.concatenate([p.astype(F32) for p in pieces(we_ref[...], 3)], axis=0).astype(BF16)
    rows[0:1, :] = jnp.sum(dot(energy_rows, wup_ref[...], NT), axis=0, keepdims=True)
    rows[1:2, :] = jnp.sum(dot(energy_rows, embedding, NT), axis=0, keepdims=True)

    pl.semaphore_wait(barrier, len(DIRS))

    def spread(n):
        role, dx, dy = DIRS[n]
        (xs, xe), (ys_, ye) = own_part(dx), own_part(dy)
        (tx, te), (ty, tf) = halo_part(-dx), halo_part(-dy)
        return pltpu.make_async_remote_copy(
            src_ref=pad.at[CENTRE, 1 + xs : 1 + xe, 1 + ys_ : 1 + ye],
            dst_ref=pad.at[role, tx:te, ty:tf],
            send_sem=send1.at[n],
            recv_sem=recv1.at[n],
            device_id=device(role, dx, dy),
            device_id_type=MESH,
        )

    out_copies = [spread(n) for n in range(len(DIRS))]
    for copy in out_copies:
        copy.start()

    lane2 = lax.broadcasted_iota(jnp.int32, (2, 128), 1)
    low2 = lane2 < SLOTS
    first2 = lax.broadcasted_iota(jnp.int32, (2, 128), 0) == 0
    species_row = lax.broadcasted_iota(jnp.int32, (SPEC, 128), 0).astype(F32)
    toward = (1 - 2 * odd).astype(F32)
    zoff = (jnp.zeros((), F32), toward, -toward)

    def pair_tile(t, cell_a, cell_b):
        (ra, xa, ya), (rb, xb, yb) = cell_a, cell_b
        a, b = pad[ra, xa, ya], pad[rb, xb, yb]
        a_swapped, b_swapped = pltpu.roll(a, SLOTS, 1), pltpu.roll(b, SLOTS, 1)
        offset = jnp.where(
            first2, jnp.where(low2, float(xa), float(xb)), jnp.where(low2, zoff[ra], zoff[rb])
        )
        xz[t] = jnp.where(low2, a, b_swapped) + offset
        mixed = jnp.where(low2, a_swapped, b)
        ys[t] = mixed + jnp.where(first2, jnp.where(low2, float(ya), float(yb)), 0.0)
        hot[t] = jnp.where(species_row == mixed[1:2, :], 1.0, 0.0).astype(BF16)

    def geometry(c, t, lo, size):
        dx = xz[t, 0:1, :] - anchor[c, 0, lo : lo + size, :]
        dy = ys[t, 0:1, :] - anchor[c, 1, lo : lo + size, :]
        dz = xz[t, 1:2, :] - anchor[c, 2, lo : lo + size, :]
        dist_sq = dx * dx + dy * dy + dz * dz
        falloff = jnp.maximum(1.0 - dist_sq, 0.0)
        return dx, dy, dz, falloff, jnp.exp(-0.5 * dist_sq)

    def weight_sums(c, tiles):
        for n, t in enumerate(tiles):
            for lo in range(0, SLOTS, 16):
                _, _, _, falloff, e0 = geometry(c, t, lo, 16)
                square = falloff * falloff
                if t == (1 + c // 2) * 4 + 1 + c % 2:
                    i = lax.broadcasted_iota(jnp.int32, (16, 128), 0) + lo
                    j = lax.broadcasted_iota(jnp.int32, (16, 128), 1)
                    square = jnp.where(i == j, 0.0, square)
                w = e0 * square
                u = e0 * e0
                u3 = u * u * u
                ladder = (u, u3, u3 * u3 * u3)
                for k in range(RAD):
                    wbuf[c, k * SLOTS + lo : k * SLOTS + lo + 16, n * 128 : (n + 1) * 128] = w.astype(BF16)
                    if k < RAD - 1:
                        w = w * ladder[k]
        onehot = jnp.concatenate([hot[t] for t in tiles], axis=1)
        return dot(wbuf[c, :, 0 : len(tiles) * 128], onehot, NT)

    def pair_forces(c, tiles, first):
        own = [[None] * (SLOTS // 8) for _ in range(3)]
        for t in tiles:
            onehot = hot[t]
            gathered = dot(abuf[c], jnp.concatenate([onehot, onehot], axis=0))
            other = [None] * 3
            for r in range(SLOTS // 8):
                dx, dy, dz, falloff, e0 = geometry(c, t, 8 * r, 8)
                u = e0 * e0
                u3 = u * u * u
                e1 = e0 * u
                e2 = e1 * u3
                e3 = e2 * (u3 * u3 * u3)
                q0, q1, q2, q3 = (
                    e * gathered[k * SLOTS + 8 * r : k * SLOTS + 8 * r + 8, :]
                    for k, e in enumerate((e0, e1, e2, e3))
                )
                plain = (q0 + q1) + (q2 + q3)
                graded = q0 + 3.0 * (q1 + 3.0 * (q2 + 3.0 * q3))
                pair = falloff * (falloff * graded + 4.0 * plain)
                for q, delta in enumerate((dx, dy, dz)):
                    term = pair * delta
                    own[q][r] = term if own[q][r] is None else own[q][r] + term
                    other[q] = term if other[q] is None else other[q] + term
            for q in range(3):
                racc[t, q] = racc[t, q] + other[q]
        for q in range(3):
            for r in range(SLOTS // 8):
                place = slice(q * SLOTS + 8 * r, q * SLOTS + 8 * r + 8)
                dacc[c, place, :] = own[q][r] if first else dacc[c, place, :] + own[q][r]

    def give_back(t, cell_a, cell_b):
        low = lax.broadcasted_iota(jnp.int32, (1, 128), 1) < SLOTS
        fx, fy, fz = (-jnp.sum(racc[t, q], axis=0, keepdims=True) for q in range(3))
        swap = lambda v: pltpu.roll(v, SLOTS, 1)
        ra, xa, ya = cell_a
        rb, xb, yb = cell_b
        back[ra, xa, ya, 0:1, :] = jnp.where(low, fx, swap(fy))
        back[ra, xa, ya, 1:2, :] = jnp.where(low, fz, 0.0)
        back[rb, xb, yb, 0:1, :] = jnp.where(low, swap(fx), fy)
        back[rb, xb, yb, 1:2, :] = jnp.where(low, swap(fz), 0.0)

    def collect(n):
        role, dx, dy = DIRS[n]
        (xs, xe), (ys_, ye) = halo_part(dx), halo_part(dy)
        return pltpu.make_async_remote_copy(
            src_ref=back.at[role, xs:xe, ys_:ye],
            dst_ref=rec.at[n, 0 : xe - xs, 0 : ye - ys_],
            send_sem=send2.at[n],
            recv_sem=recv2.at[n],
            device_id=device(role, dx, dy),
            device_id_type=MESH,
        )

    near_pairs = [(x * 4 + y, (CENTRE, x, y), (NEAR, x, y)) for x in range(4) for y in range(4)]
    far_pairs = [
        (16 + h * 4 + y, (FAR, 2 * h, y), (FAR, 2 * h + 1, y)) for h in range(2) for y in range(4)
    ]
    racc[...] = jnp.zeros_like(racc)

    for n, d in enumerate(DIRS):
        if d[0] != FAR:
            out_copies[n].wait_recv()
    for pair in near_pairs:
        pair_tile(*pair)
    for c in range(4):
        sbuf[c] = weight_sums(c, near_tiles(c))

    for n, d in enumerate(DIRS):
        if d[0] == FAR:
            out_copies[n].wait_recv()
    for pair in far_pairs:
        pair_tile(*pair)
    readout = rows[0:1, :]
    slot_row = lax.broadcasted_iota(jnp.int32, (SLOTS, CH), 0)
    for c in range(4):
        sums = sbuf[c] + weight_sums(c, far_tiles(c))
        wide = jnp.concatenate([sums[k * SLOTS : (k + 1) * SLOTS, :] for k in range(RAD)], axis=1)
        high, rest = pieces(wide, 2)
        both = dot(jnp.concatenate([high, rest], axis=0), table[...])
        message = MSG_SCALE * (both[0:SLOTS, :] + both[SLOTS : 2 * SLOTS, :])
        sigmoid = 1.0 / (1.0 + jnp.exp(-message))
        act[c] = (message * sigmoid).astype(BF16)
        occupied = (slot_row < cnt_ref[c]).astype(F32)
        adjoint = (occupied * sigmoid * (1.0 + message * (1.0 - sigmoid)) * readout).astype(BF16)
        slopes = -MSG_SCALE * dot(adjoint, table[...], NT)
        slopes = jnp.concatenate([slopes[:, k * SPEC : (k + 1) * SPEC] for k in range(RAD)], axis=0)
        abuf[c] = jnp.concatenate(pieces(slopes, 2), axis=1)
        pair_forces(c, far_tiles(c), True)
    for pair in far_pairs:
        give_back(*pair)
    back_copies = [collect(n) for n in range(len(DIRS))]
    for n, d in enumerate(DIRS):
        if d[0] == FAR:
            back_copies[n].start()
    for c in range(4):
        pair_forces(c, near_tiles(c), False)
    for pair in near_pairs:
        give_back(*pair)
    for n, d in enumerate(DIRS):
        if d[0] != FAR:
            back_copies[n].start()

    occupied_rows = [(slot_lane < cnt_ref[c]).astype(F32) for c in range(4)]
    readout_rows = jnp.concatenate([p.astype(F32) for p in pieces(rows[0:1, :], 3)], axis=0).astype(BF16)
    species_rows = jnp.concatenate([p.astype(F32) for p in pieces(rows[1:2, :], 3)], axis=0).astype(BF16)
    for c in range(4):
        centre = hot[(1 + c // 2) * 4 + 1 + c % 2]
        parts = dot(readout_rows, act[c], NT) + dot(species_rows, centre)[:, 0:SLOTS]
        en_ref[c : c + 1, :] = occupied_rows[c] * jnp.sum(parts, axis=0, keepdims=True)
    ones = jnp.ones((8, 128), F32)
    own = [dot(ones, dacc[c], NT, lax.Precision.HIGHEST)[0:1, :] for c in range(4)]
    for copy in back_copies:
        copy.wait_recv()
    for c in range(4):
        x, y = c // 2, c % 2
        total = back[CENTRE, 1 + x, 1 + y]
        for n, (role, dx, dy) in enumerate(DIRS):
            (xs, xe), (ys_, ye) = own_part(-dx), own_part(-dy)
            if xs <= x < xe and ys_ <= y < ye:
                total = total + rec[n, x - xs, y - ys_]
        planar = own[c][:, 0:128] + total[0:1, :]
        upright = own[c][:, 128:192] + total[1:2, 0:SLOTS]
        mask = occupied_rows[c]
        fo_ref[c : c + 1, 0:128] = planar * jnp.concatenate([mask, mask], axis=1)
        fo_ref[c : c + 1, 128:192] = upright * mask
    for copy in out_copies:
        copy.wait_send()
    for copy in back_copies:
        copy.wait_send()


def solution(mesh):
    sizes = tuple(mesh.shape[name] for name in ("gx", "gy", "gz"))
    in_specs = (
        P("gx", "gy", "gz", None),
        P("gx", "gy", "gz", None),
        P("gx", "gy", "gz"),
        P(),
        P(),
        P(),
        P(),
    )
    out_specs = (P("gx", "gy", "gz", None), P("gx", "gy", "gz", None))
    vmem = pl.BlockSpec(memory_space=pltpu.VMEM)
    smem = pl.BlockSpec(memory_space=pltpu.SMEM)
    count = len(DIRS)

    def on_device(positions, species, counts, embed, filters, w_up, w_energy):
        energies, forces = pl.pallas_call(
            functools.partial(kernel, sizes),
            out_shape=(
                jax.ShapeDtypeStruct((4, SLOTS), F32),
                jax.ShapeDtypeStruct((4, 3 * SLOTS), F32),
            ),
            in_specs=[smem] + [vmem] * 6,
            out_specs=(vmem, vmem),
            scratch_shapes=[
                pltpu.VMEM((3, 4, 4, 2, 128), F32),
                pltpu.VMEM((count, 2, 2, 2, 128), F32),
                pltpu.VMEM((3, 4, 4, 2, 128), F32),
                pltpu.VMEM((24, 2, 128), F32),
                pltpu.VMEM((24, 2, 128), F32),
                pltpu.VMEM((24, SPEC, 128), BF16),
                pltpu.VMEM((4, 3, SLOTS, 128), F32),
                pltpu.VMEM((RAD * SPEC, CH), BF16),
                pltpu.VMEM((8, 128), F32),
                pltpu.VMEM((SPEC, CH), F32),
                pltpu.VMEM((4, RAD * SLOTS, 9 * 128), BF16),
                pltpu.VMEM((4, RAD * SLOTS, SPEC), F32),
                pltpu.VMEM((4, RAD * SLOTS, 2 * SPEC), BF16),
                pltpu.VMEM((4, SLOTS, CH), BF16),
                pltpu.VMEM((24, 3, 8, 128), F32),
                pltpu.VMEM((4, 3 * SLOTS, 128), F32),
                pltpu.SemaphoreType.DMA((count,)),
                pltpu.SemaphoreType.DMA((count,)),
                pltpu.SemaphoreType.DMA((count,)),
                pltpu.SemaphoreType.DMA((count,)),
            ],
            compiler_params=pltpu.CompilerParams(
                collective_id=0, has_side_effects=True, vmem_limit_bytes=48 * 1024 * 1024
            ),
        )(
            counts.reshape(4),
            positions.reshape(4, 3 * SLOTS),
            species.reshape(4, SLOTS),
            embed,
            filters,
            w_up,
            w_energy.reshape(1, CH),
        )
        return energies.reshape(species.shape), forces.reshape(positions.shape)

    return jax.shard_map(
        on_device, mesh=mesh, in_specs=in_specs, out_specs=out_specs, check_vma=False
    )
```

```python
import functools

import jax
import jax.numpy as jnp
from jax import lax
from jax.experimental import pallas as pl
from jax.experimental.pallas import tpu as pltpu
from jax.sharding import PartitionSpec as P

MESH = pl.DeviceIdType.MESH
F32 = jnp.float32
BF16 = jnp.bfloat16

SLOTS = 64
CH = 128
RAD = 4
SPEC = 128
MSG_SCALE = 0.1
LOG2E = 1.4426950408889634
HALF = 0.5

CENTRE, NEAR, FAR = 0, 1, 2
NT = (((1,), (1,)), ((), ()))
NN = (((1,), (0,)), ((), ()))

DIRS = [
    (role, dx, dy)
    for role in (FAR, CENTRE, NEAR)
    for dx, dy in ((1, 1), (1, -1), (-1, 1), (-1, -1), (0, 1), (0, -1), (1, 0), (-1, 0), (0, 0))
    if (role, dx, dy) != (CENTRE, 0, 0)
]


def dot(a, b, dims=NN, precision=None):
    return lax.dot_general(a, b, dims, precision=precision, preferred_element_type=F32)


def pieces(values, count):
    out = []
    for _ in range(count):
        out.append(values.astype(BF16))
        values = values - out[-1].astype(F32)
    return out


def own_part(step):
    return {1: (1, 2), -1: (0, 1), 0: (0, 2)}[step]


def halo_part(step):
    return {1: (3, 4), -1: (0, 1), 0: (1, 3)}[step]


OWN_COLUMNS = [(x, y) for x in (1, 2) for y in (1, 2)]
PLANE_PAIRS = [((CENTRE, x, y), (NEAR, x, y)) for x in range(4) for y in range(4)]
FAR_PAIRS = [
    ((FAR,) + a, (FAR,) + b)
    for a, b in (
        ((0, 0), (1, 0)),
        ((2, 0), (3, 0)),
        ((3, 1), (3, 2)),
        ((3, 3), (2, 3)),
        ((1, 3), (0, 3)),
        ((0, 2), (0, 1)),
        ((1, 1), (1, 2)),
        ((2, 1), (2, 2)),
    )
]
PAIRS = PLANE_PAIRS + FAR_PAIRS


def tiles_of(c, wanted):
    x, y = 1 + c // 2, 1 + c % 2
    return [
        t
        for t, pair in enumerate(PAIRS)
        if wanted(pair) and any(abs(a - x) <= 1 and abs(b - y) <= 1 for _, a, b in pair)
    ]


def is_own(pair):
    return pair[0][0] != FAR and pair[0][1:] in OWN_COLUMNS


def is_side(pair):
    return pair[0][0] != FAR and pair[0][1:] not in OWN_COLUMNS


def is_far(pair):
    return pair[0][0] == FAR


def is_far_core(pair):
    return is_far(pair) and pair[0][1:] in OWN_COLUMNS


def is_far_ring(pair):
    return is_far(pair) and not is_far_core(pair)


def kernel(
    sizes,
    pos_hbm,
    spec_hbm,
    cnt_hbm,
    embed_hbm,
    filt_hbm,
    wup_hbm,
    we_hbm,
    en_ref,
    fo_ref,
    pos_ref,
    spec_ref,
    cnt_ref,
    embed_ref,
    filt_ref,
    wup_ref,
    we_ref,
    fetch,
    pad,
    rec,
    back,
    xz,
    ys,
    hot,
    anchor,
    table,
    rows,
    emb,
    sbuf,
    abuf,
    act,
    racc,
    dacc,
    send1,
    recv1,
    send2,
    recv2,
):
    nx, ny, nz = sizes
    gx, gy, gz = (lax.axis_index(name) for name in ("gx", "gy", "gz"))
    odd = lax.rem(gz, 2)
    roles = (gz, gz + 1 - 2 * odd, lax.rem(gz + nz - 1 + 2 * odd, nz))

    def device(role, dx, dy):
        return (lax.rem(gx + nx + dx, nx), lax.rem(gy + ny + dy, ny), roles[role])

    operands = [
        (pos_hbm, pos_ref),
        (spec_hbm, spec_ref),
        (cnt_hbm, cnt_ref),
        (embed_hbm, embed_ref),
        (filt_hbm, filt_ref),
        (wup_hbm, wup_ref),
        (we_hbm, we_ref),
    ]
    loads = [pltpu.make_async_copy(a, b, fetch.at[n]) for n, (a, b) in enumerate(operands)]
    for load in loads[0:3]:
        load.start()
    barrier = pltpu.get_barrier_semaphore()
    for d in DIRS:
        pl.semaphore_signal(barrier, inc=1, device_id=device(*d), device_id_type=MESH)
    for load in loads[3:]:
        load.start()
    for load in loads[0:3]:
        load.wait()

    slot_lane = lax.broadcasted_iota(jnp.int32, (1, SLOTS), 1)
    counts = [cnt_ref[c // 2, 0:1, c % 2 : c % 2 + 1] for c in range(4)]
    places = [pos_ref.at[c // 2, c % 2] for c in range(4)]
    for c in range(4):
        marked = jnp.where(slot_lane < counts[c], spec_ref[c // 2, c % 2], -1).astype(F32)
        pad[CENTRE, 1 + c // 2, 1 + c % 2, 0:1, :] = places[c][:, 0:128]
        pad[CENTRE, 1 + c // 2, 1 + c % 2, 1:2, :] = jnp.concatenate(
            [places[c][:, 128:192], marked], axis=1
        )
    eye = lax.broadcasted_iota(jnp.int32, (SLOTS, SLOTS), 0) == lax.broadcasted_iota(
        jnp.int32, (SLOTS, SLOTS), 1
    )
    for c in range(4):
        for q in range(3):
            row = jnp.broadcast_to(places[c][:, q * SLOTS : (q + 1) * SLOTS], (SLOTS, SLOTS))
            column = jnp.sum(jnp.where(eye, row, 0.0), axis=1, keepdims=True)
            shift = (1.0 + c // 2, 1.0 + c % 2, 0.0)[q]
            anchor[c, q] = jnp.broadcast_to(HALF * (column + shift), (SLOTS, 128))
    for load in loads[3:]:
        load.wait()
    emb[...] = jnp.zeros_like(emb)
    emb[0 : embed_ref.shape[0], :] = embed_ref[...].astype(F32)
    embedding = emb[...].astype(BF16)
    for k in range(RAD):
        table[k * SPEC : (k + 1) * SPEC, :] = dot(
            embedding, filt_ref[:, k * CH : (k + 1) * CH]
        ).astype(BF16)
    energy_rows = jnp.concatenate([p.astype(F32) for p in pieces(we_ref[...], 3)], axis=0).astype(BF16)
    rows[0:1, :] = jnp.sum(dot(energy_rows, wup_ref[...], NT), axis=0, keepdims=True)
    rows[1:2, :] = jnp.sum(dot(energy_rows, embedding, NT), axis=0, keepdims=True)

    pl.semaphore_wait(barrier, len(DIRS))

    def spread(n):
        role, dx, dy = DIRS[n]
        (xs, xe), (ys_, ye) = own_part(dx), own_part(dy)
        (tx, te), (ty, tf) = halo_part(-dx), halo_part(-dy)
        return pltpu.make_async_remote_copy(
            src_ref=pad.at[CENTRE, 1 + xs : 1 + xe, 1 + ys_ : 1 + ye],
            dst_ref=pad.at[role, tx:te, ty:tf],
            send_sem=send1.at[n],
            recv_sem=recv1.at[n],
            device_id=device(role, dx, dy),
            device_id_type=MESH,
        )

    out_copies = [spread(n) for n in range(len(DIRS))]
    for copy in out_copies:
        copy.start()

    lane2 = lax.broadcasted_iota(jnp.int32, (2, 128), 1)
    low2 = lane2 < SLOTS
    first2 = lax.broadcasted_iota(jnp.int32, (2, 128), 0) == 0
    species_row = lax.broadcasted_iota(jnp.int32, (SPEC, 128), 0).astype(F32)
    toward = (1 - 2 * odd).astype(F32)
    zoff = (jnp.zeros((), F32), toward, -toward)

    def pair_tile(t, cell_a, cell_b):
        (ra, xa, ya), (rb, xb, yb) = cell_a, cell_b
        a, b = pad[ra, xa, ya], pad[rb, xb, yb]
        a_swapped, b_swapped = pltpu.roll(a, SLOTS, 1), pltpu.roll(b, SLOTS, 1)
        offset = jnp.where(
            first2, jnp.where(low2, float(xa), float(xb)), jnp.where(low2, zoff[ra], zoff[rb])
        )
        xz[t] = HALF * (jnp.where(low2, a, b_swapped) + offset)
        mixed = jnp.where(low2, a_swapped, b)
        ys[t] = HALF * (mixed + jnp.where(first2, jnp.where(low2, float(ya), float(yb)), 0.0))
        hot[t] = jnp.where(species_row == mixed[1:2, :], 1.0, 0.0).astype(BF16)

    def geometry(c, t, lo, size):
        dx = xz[t, 0:1, :] - anchor[c, 0, lo : lo + size, :]
        dy = ys[t, 0:1, :] - anchor[c, 1, lo : lo + size, :]
        dz = xz[t, 1:2, :] - anchor[c, 2, lo : lo + size, :]
        dist_sq = dx * dx + dy * dy + dz * dz
        falloff = jnp.maximum(HALF * HALF - dist_sq, 0.0)
        decaying = [jnp.exp2((-0.5 * LOG2E * 3.0**k / HALF**2) * dist_sq) for k in range(RAD)]
        return dx, dy, dz, falloff, decaying

    def weight_sums(c, tiles):
        columns = []
        for t in tiles:
            blocks = [[] for _ in range(RAD)]
            for lo in range(0, SLOTS, 16):
                _, _, _, falloff, decaying = geometry(c, t, lo, 16)
                square = falloff * falloff
                if t == (1 + c // 2) * 4 + 1 + c % 2:
                    i = lax.broadcasted_iota(jnp.int32, (16, 128), 0) + lo
                    j = lax.broadcasted_iota(jnp.int32, (16, 128), 1)
                    square = jnp.where(i == j, 0.0, square)
                for k in range(RAD):
                    blocks[k].append((decaying[k] * square).astype(BF16))
            columns.append(jnp.concatenate(sum(blocks, []), axis=0))
        onehot = jnp.concatenate([hot[t] for t in tiles], axis=1)
        return dot(jnp.concatenate(columns, axis=1), onehot, NT)

    def pair_forces(c, tiles, first):
        own = [[None] * (SLOTS // 8) for _ in range(3)]
        for start in range(0, len(tiles), 2):
            group = tiles[start : start + 2]
            onehot = jnp.concatenate([hot[t] for t in group], axis=1)
            gathered = dot(abuf[c], jnp.concatenate([onehot, onehot], axis=0))
            for n, t in enumerate(group):
                other = [None] * 3
                for r in range(SLOTS // 8):
                    dx, dy, dz, falloff, decaying = geometry(c, t, 8 * r, 8)
                    q0, q1, q2, q3 = (
                        e * gathered[k * SLOTS + 8 * r : k * SLOTS + 8 * r + 8, n * 128 : (n + 1) * 128]
                        for k, e in enumerate(decaying)
                    )
                    plain = (q0 + q1) + (q2 + q3)
                    graded = q0 + 3.0 * (q1 + 3.0 * (q2 + 3.0 * q3))
                    pair = falloff * (falloff * graded + plain)
                    for q, delta in enumerate((dx, dy, dz)):
                        term = pair * delta
                        own[q][r] = term if own[q][r] is None else own[q][r] + term
                        other[q] = term if other[q] is None else other[q] + term
                for q in range(3):
                    racc[t, q] = racc[t, q] + other[q]
        for q in range(3):
            for r in range(SLOTS // 8):
                place = slice(q * SLOTS + 8 * r, q * SLOTS + 8 * r + 8)
                dacc[c, place, :] = own[q][r] if first else dacc[c, place, :] + own[q][r]

    def give_back(t, cell_a, cell_b):
        low = lax.broadcasted_iota(jnp.int32, (1, 128), 1) < SLOTS
        fx, fy, fz = (-jnp.sum(racc[t, q], axis=0, keepdims=True) for q in range(3))
        swap = lambda v: pltpu.roll(v, SLOTS, 1)
        ra, xa, ya = cell_a
        rb, xb, yb = cell_b
        back[ra, xa, ya, 0:1, :] = jnp.where(low, fx, swap(fy))
        back[ra, xa, ya, 1:2, :] = jnp.where(low, fz, 0.0)
        back[rb, xb, yb, 0:1, :] = jnp.where(low, swap(fx), fy)
        back[rb, xb, yb, 1:2, :] = jnp.where(low, swap(fz), 0.0)

    def collect(n):
        role, dx, dy = DIRS[n]
        (xs, xe), (ys_, ye) = halo_part(dx), halo_part(dy)
        return pltpu.make_async_remote_copy(
            src_ref=back.at[role, xs:xe, ys_:ye],
            dst_ref=rec.at[n, 0 : xe - xs, 0 : ye - ys_],
            send_sem=send2.at[n],
            recv_sem=recv2.at[n],
            device_id=device(role, dx, dy),
            device_id_type=MESH,
        )

    racc[...] = jnp.zeros_like(racc)
    own_tiles = [tiles_of(c, is_own) for c in range(4)]
    side_tiles = [tiles_of(c, is_side) for c in range(4)]
    far_tiles = [tiles_of(c, is_far) for c in range(4)]

    mate = (NEAR, 0, 0)
    out_copies[DIRS.index(mate)].wait_recv()
    for t, pair in enumerate(PAIRS):
        if is_own(pair):
            pair_tile(t, *pair)
    for c in range(4):
        sbuf[c] = weight_sums(c, own_tiles[c])

    for n, d in enumerate(DIRS):
        if d[0] != FAR and d != mate:
            out_copies[n].wait_recv()
    for t, pair in enumerate(PAIRS):
        if is_side(pair):
            pair_tile(t, *pair)
    for c in range(4):
        sbuf[c] = sbuf[c] + weight_sums(c, side_tiles[c])

    for n, d in enumerate(DIRS):
        if d[0] == FAR:
            out_copies[n].wait_recv()
    for t, pair in enumerate(PAIRS):
        if is_far(pair):
            pair_tile(t, *pair)
    readout = rows[0:1, :]
    slot_row = lax.broadcasted_iota(jnp.int32, (SLOTS, CH), 0)
    for c in range(4):
        sbuf[c] = sbuf[c] + weight_sums(c, far_tiles[c])
    for c in range(4):
        sums = sbuf[c]
        wide = jnp.concatenate([sums[k * SLOTS : (k + 1) * SLOTS, :] for k in range(RAD)], axis=1)
        high, rest = pieces(wide, 2)
        both = dot(jnp.concatenate([high, rest], axis=0), table[...])
        message = (MSG_SCALE / HALF**4) * (both[0:SLOTS, :] + both[SLOTS : 2 * SLOTS, :])
        sigmoid = 1.0 / (1.0 + jnp.exp(-message))
        act[c] = (message * sigmoid).astype(BF16)
        occupied = (slot_row < counts[c]).astype(F32)
        adjoint = (occupied * sigmoid * (1.0 + message * (1.0 - sigmoid)) * readout).astype(BF16)
        slopes = (-MSG_SCALE * 4 / HALF**3) * dot(adjoint, table[...], NT)
        slopes = jnp.concatenate([slopes[:, k * SPEC : (k + 1) * SPEC] for k in range(RAD)], axis=0)
        abuf[c] = jnp.concatenate(pieces(slopes, 2), axis=1)
    back_copies = [collect(n) for n in range(len(DIRS))]

    def react(wanted, sends, first=False):
        for c in range(4):
            pair_forces(c, tiles_of(c, wanted), first)
        for t, pair in enumerate(PAIRS):
            if wanted(pair):
                give_back(t, *pair)
        for n, d in enumerate(DIRS):
            if sends(d):
                back_copies[n].start()

    react(is_far_ring, lambda d: d[0] == FAR and d[1:] != (0, 0), True)
    react(is_side, lambda d: d[0] != FAR and d[1:] != (0, 0))
    react(is_far_core, lambda d: d == (FAR, 0, 0))
    react(is_own, lambda d: d == (NEAR, 0, 0))

    occupied_rows = [(slot_lane < counts[c]).astype(F32) for c in range(4)]
    readout_rows = jnp.concatenate([p.astype(F32) for p in pieces(rows[0:1, :], 3)], axis=0).astype(BF16)
    species_rows = jnp.concatenate([p.astype(F32) for p in pieces(rows[1:2, :], 3)], axis=0).astype(BF16)
    for c in range(4):
        centre = hot[(1 + c // 2) * 4 + 1 + c % 2]
        parts = dot(readout_rows, act[c], NT) + dot(species_rows, centre)[:, 0:SLOTS]
        en_ref[c // 2, c % 2] = occupied_rows[c] * jnp.sum(parts, axis=0, keepdims=True)
    ones = jnp.ones((8, 128), F32)
    own = [dot(ones, dacc[c], NT, lax.Precision.HIGHEST)[0:1, :] for c in range(4)]
    for copy in back_copies:
        copy.wait_recv()
    for c in range(4):
        x, y = c // 2, c % 2
        total = back[CENTRE, 1 + x, 1 + y]
        for n, (role, dx, dy) in enumerate(DIRS):
            (xs, xe), (ys_, ye) = own_part(-dx), own_part(-dy)
            if xs <= x < xe and ys_ <= y < ye:
                total = total + rec[n, x - xs, y - ys_]
        planar = own[c][:, 0:128] + total[0:1, :]
        upright = own[c][:, 128:192] + total[1:2, 0:SLOTS]
        mask = occupied_rows[c]
        fo_ref[c // 2, c % 2, :, 0:128] = planar * jnp.concatenate([mask, mask], axis=1)
        fo_ref[c // 2, c % 2, :, 128:192] = upright * mask
    for copy in out_copies:
        copy.wait_send()
    for copy in back_copies:
        copy.wait_send()


def solution(mesh):
    sizes = tuple(mesh.shape[name] for name in ("gx", "gy", "gz"))
    in_specs = (
        P("gx", "gy", "gz", None),
        P("gx", "gy", "gz", None),
        P("gx", "gy", "gz"),
        P(),
        P(),
        P(),
        P(),
    )
    out_specs = (P("gx", "gy", "gz", None), P("gx", "gy", "gz", None))
    vmem = pl.BlockSpec(memory_space=pltpu.VMEM)
    anywhere = pl.BlockSpec(memory_space=pl.ANY)
    count = len(DIRS)

    def on_device(positions, species, counts, embed, filters, w_up, w_energy):
        operands = (
            positions,
            species,
            counts.transpose(0, 2, 1),
            embed,
            filters,
            w_up,
            w_energy.reshape(1, CH),
        )
        operands = [pltpu.with_memory_space_constraint(a, pltpu.HBM) for a in operands]
        return pl.pallas_call(
            functools.partial(kernel, sizes),
            out_shape=(
                jax.ShapeDtypeStruct(species.shape, F32),
                jax.ShapeDtypeStruct(positions.shape, F32),
            ),
            in_specs=[anywhere] * len(operands),
            out_specs=(vmem, vmem),
            scratch_shapes=[pltpu.VMEM(a.shape, a.dtype) for a in operands]
            + [
                pltpu.SemaphoreType.DMA((len(operands),)),
                pltpu.VMEM((3, 4, 4, 2, 128), F32),
                pltpu.VMEM((count, 2, 2, 2, 128), F32),
                pltpu.VMEM((3, 4, 4, 2, 128), F32),
                pltpu.VMEM((24, 2, 128), F32),
                pltpu.VMEM((24, 2, 128), F32),
                pltpu.VMEM((24, SPEC, 128), BF16),
                pltpu.VMEM((4, 3, SLOTS, 128), F32),
                pltpu.VMEM((RAD * SPEC, CH), BF16),
                pltpu.VMEM((8, 128), F32),
                pltpu.VMEM((SPEC, CH), F32),
                pltpu.VMEM((4, RAD * SLOTS, SPEC), F32),
                pltpu.VMEM((4, RAD * SLOTS, 2 * SPEC), BF16),
                pltpu.VMEM((4, SLOTS, CH), BF16),
                pltpu.VMEM((24, 3, 8, 128), F32),
                pltpu.VMEM((4, 3 * SLOTS, 128), F32),
                pltpu.SemaphoreType.DMA((count,)),
                pltpu.SemaphoreType.DMA((count,)),
                pltpu.SemaphoreType.DMA((count,)),
                pltpu.SemaphoreType.DMA((count,)),
            ],
            compiler_params=pltpu.CompilerParams(
                collective_id=0, has_side_effects=True, vmem_limit_bytes=48 * 1024 * 1024
            ),
        )(*operands)

    return jax.shard_map(
        on_device, mesh=mesh, in_specs=in_specs, out_specs=out_specs, check_vma=False
    )
```

```python
import functools

import jax
import jax.numpy as jnp
from jax import lax
from jax.experimental import pallas as pl
from jax.experimental.pallas import tpu as pltpu
from jax.sharding import PartitionSpec as P

MESH = pl.DeviceIdType.MESH
F32 = jnp.float32
BF16 = jnp.bfloat16

SLOTS = 64
CH = 128
RAD = 4
SPEC = 128
MSG_SCALE = 0.1
LOG2E = 1.4426950408889634
HALF = 0.5

FORCE_SCALE = -MSG_SCALE * 4 / HALF**3

CENTRE, NEAR, FAR = 0, 1, 2
NT = (((1,), (1,)), ((), ()))
NN = (((1,), (0,)), ((), ()))

DIRS = [
    (role, dx, dy)
    for role in (FAR, CENTRE, NEAR)
    for dx, dy in ((1, 1), (1, -1), (-1, 1), (-1, -1), (0, 1), (0, -1), (1, 0), (-1, 0), (0, 0))
    if (role, dx, dy) != (CENTRE, 0, 0)
]


def dot(a, b, dims=NN, precision=None):
    return lax.dot_general(a, b, dims, precision=precision, preferred_element_type=F32)


def pieces(values, count):
    out = []
    for _ in range(count):
        out.append(values.astype(BF16))
        values = values - out[-1].astype(F32)
    return out


def own_part(step):
    return {1: (1, 2), -1: (0, 1), 0: (0, 2)}[step]


def halo_part(step):
    return {1: (3, 4), -1: (0, 1), 0: (1, 3)}[step]


OWN_COLUMNS = [(x, y) for x in (1, 2) for y in (1, 2)]
PLANE_PAIRS = [((CENTRE, x, y), (NEAR, x, y)) for x in range(4) for y in range(4)]
FAR_PAIRS = [
    ((FAR,) + a, (FAR,) + b)
    for a, b in (
        ((0, 0), (1, 0)),
        ((2, 0), (3, 0)),
        ((3, 1), (3, 2)),
        ((3, 3), (2, 3)),
        ((1, 3), (0, 3)),
        ((0, 2), (0, 1)),
        ((1, 1), (1, 2)),
        ((2, 1), (2, 2)),
    )
]
PAIRS = PLANE_PAIRS + FAR_PAIRS


def tiles_of(c, wanted):
    x, y = 1 + c // 2, 1 + c % 2
    return [
        t
        for t, pair in enumerate(PAIRS)
        if wanted(pair) and any(abs(a - x) <= 1 and abs(b - y) <= 1 for _, a, b in pair)
    ]


def is_own(pair):
    return pair[0][0] != FAR and pair[0][1:] in OWN_COLUMNS


def is_side(pair):
    return pair[0][0] != FAR and pair[0][1:] not in OWN_COLUMNS


def is_far(pair):
    return pair[0][0] == FAR


def is_far_core(pair):
    return is_far(pair) and pair[0][1:] in OWN_COLUMNS


def is_far_ring(pair):
    return is_far(pair) and not is_far_core(pair)


def corner_of(c):
    cell = (FAR, 3 * (c // 2), 3 * (c % 2))
    return next((t, pair.index(cell)) for t, pair in enumerate(PAIRS) if cell in pair)


def kernel(
    sizes,
    pos_hbm,
    spec_hbm,
    cnt_hbm,
    embed_hbm,
    filt_hbm,
    wup_hbm,
    we_hbm,
    en_ref,
    fo_ref,
    pos_ref,
    spec_ref,
    cnt_ref,
    embed_ref,
    filt_ref,
    wup_ref,
    we_ref,
    fetch,
    pad,
    rec,
    back,
    xz,
    ys,
    hot,
    anchor,
    table,
    rows,
    emb,
    sbuf,
    abuf,
    act,
    racc,
    dacc,
    send1,
    recv1,
    send2,
    recv2,
):
    nx, ny, nz = sizes
    gx, gy, gz = (lax.axis_index(name) for name in ("gx", "gy", "gz"))
    odd = lax.rem(gz, 2)
    roles = (gz, gz + 1 - 2 * odd, lax.rem(gz + nz - 1 + 2 * odd, nz))

    def device(role, dx, dy):
        return (lax.rem(gx + nx + dx, nx), lax.rem(gy + ny + dy, ny), roles[role])

    operands = [
        (pos_hbm, pos_ref),
        (spec_hbm, spec_ref),
        (cnt_hbm, cnt_ref),
        (embed_hbm, embed_ref),
        (filt_hbm, filt_ref),
        (wup_hbm, wup_ref),
        (we_hbm, we_ref),
    ]
    loads = [pltpu.make_async_copy(a, b, fetch.at[n]) for n, (a, b) in enumerate(operands)]
    for load in loads[0:3]:
        load.start()
    barrier = pltpu.get_barrier_semaphore()
    for d in DIRS:
        pl.semaphore_signal(barrier, inc=1, device_id=device(*d), device_id_type=MESH)
    for load in loads[3:]:
        load.start()
    for load in loads[0:3]:
        load.wait()

    slot_lane = lax.broadcasted_iota(jnp.int32, (1, SLOTS), 1)
    counts = [cnt_ref[c // 2, 0:1, c % 2 : c % 2 + 1] for c in range(4)]
    places = [pos_ref.at[c // 2, c % 2] for c in range(4)]
    for c in range(4):
        marked = jnp.where(slot_lane < counts[c], spec_ref[c // 2, c % 2], -1).astype(F32)
        pad[CENTRE, 1 + c // 2, 1 + c % 2, 0:1, :] = places[c][:, 0:128]
        pad[CENTRE, 1 + c // 2, 1 + c % 2, 1:2, :] = jnp.concatenate(
            [places[c][:, 128:192], marked], axis=1
        )
    eye = lax.broadcasted_iota(jnp.int32, (SLOTS, SLOTS), 0) == lax.broadcasted_iota(
        jnp.int32, (SLOTS, SLOTS), 1
    )
    for c in range(4):
        for q in range(3):
            row = jnp.broadcast_to(places[c][:, q * SLOTS : (q + 1) * SLOTS], (SLOTS, SLOTS))
            column = jnp.sum(jnp.where(eye, row, 0.0), axis=1, keepdims=True)
            shift = (1.0 + c // 2, 1.0 + c % 2, 0.0)[q]
            anchor[c, q] = jnp.broadcast_to(HALF * (column + shift), (SLOTS, 128))
    for load in loads[3:]:
        load.wait()
    emb[...] = jnp.zeros_like(emb)
    emb[0 : embed_ref.shape[0], :] = embed_ref[...].astype(F32)
    embedding = emb[...].astype(BF16)
    for k in range(RAD):
        table[k * SPEC : (k + 1) * SPEC, :] = dot(
            embedding, filt_ref[:, k * CH : (k + 1) * CH]
        ).astype(BF16)
    energy_rows = jnp.concatenate([p.astype(F32) for p in pieces(we_ref[...], 3)], axis=0).astype(BF16)
    rows[0:1, :] = jnp.sum(dot(energy_rows, wup_ref[...], NT), axis=0, keepdims=True)
    rows[1:2, :] = jnp.sum(dot(energy_rows, embedding, NT), axis=0, keepdims=True)

    pl.semaphore_wait(barrier, len(DIRS))

    def spread(n):
        role, dx, dy = DIRS[n]
        (xs, xe), (ys_, ye) = own_part(dx), own_part(dy)
        (tx, te), (ty, tf) = halo_part(-dx), halo_part(-dy)
        return pltpu.make_async_remote_copy(
            src_ref=pad.at[CENTRE, 1 + xs : 1 + xe, 1 + ys_ : 1 + ye],
            dst_ref=pad.at[role, tx:te, ty:tf],
            send_sem=send1.at[n],
            recv_sem=recv1.at[n],
            device_id=device(role, dx, dy),
            device_id_type=MESH,
        )

    out_copies = [spread(n) for n in range(len(DIRS))]
    for copy in out_copies:
        copy.start()

    lane2 = lax.broadcasted_iota(jnp.int32, (2, 128), 1)
    low2 = lane2 < SLOTS
    first2 = lax.broadcasted_iota(jnp.int32, (2, 128), 0) == 0
    species_row = lax.broadcasted_iota(jnp.int32, (SPEC, 128), 0).astype(F32)
    toward = (1 - 2 * odd).astype(F32)
    zoff = (jnp.zeros((), F32), toward, -toward)

    def pair_tile(t, cell_a, cell_b):
        (ra, xa, ya), (rb, xb, yb) = cell_a, cell_b
        a, b = pad[ra, xa, ya], pad[rb, xb, yb]
        a_swapped, b_swapped = pltpu.roll(a, SLOTS, 1), pltpu.roll(b, SLOTS, 1)
        offset = jnp.where(
            first2, jnp.where(low2, float(xa), float(xb)), jnp.where(low2, zoff[ra], zoff[rb])
        )
        xz[t] = HALF * (jnp.where(low2, a, b_swapped) + offset)
        mixed = jnp.where(low2, a_swapped, b)
        ys[t] = HALF * (mixed + jnp.where(first2, jnp.where(low2, float(ya), float(yb)), 0.0))
        hot[t] = jnp.where(species_row == mixed[1:2, :], 1.0, 0.0).astype(BF16)

    def geometry(c, t, lo, size):
        dx = xz[t, 0:1, :] - anchor[c, 0, lo : lo + size, :]
        dy = ys[t, 0:1, :] - anchor[c, 1, lo : lo + size, :]
        dz = xz[t, 1:2, :] - anchor[c, 2, lo : lo + size, :]
        dist_sq = dx * dx + dy * dy + dz * dz
        falloff = jnp.maximum(HALF * HALF - dist_sq, 0.0)
        decaying = [jnp.exp2((-0.5 * LOG2E * 3.0**k / HALF**2) * dist_sq) for k in range(RAD)]
        return dx, dy, dz, falloff, decaying

    def weight_sums(c, tiles):
        columns = []
        for t in tiles:
            blocks = [[] for _ in range(RAD)]
            for lo in range(0, SLOTS, 16):
                _, _, _, falloff, decaying = geometry(c, t, lo, 16)
                square = falloff * falloff
                if t == (1 + c // 2) * 4 + 1 + c % 2:
                    i = lax.broadcasted_iota(jnp.int32, (16, 128), 0) + lo
                    j = lax.broadcasted_iota(jnp.int32, (16, 128), 1)
                    square = jnp.where(i == j, 0.0, square)
                for k in range(RAD):
                    blocks[k].append((decaying[k] * square).astype(BF16))
            columns.append(jnp.concatenate(sum(blocks, []), axis=0))
        onehot = jnp.concatenate([hot[t] for t in tiles], axis=1)
        return dot(jnp.concatenate(columns, axis=1), onehot, NT)

    def pair_forces(c, tiles, first):
        own = [[None] * (SLOTS // 8) for _ in range(3)]
        for start in range(0, len(tiles), 2):
            group = tiles[start : start + 2]
            onehot = jnp.concatenate([hot[t] for t in group], axis=1)
            gathered = dot(abuf[c], jnp.concatenate([onehot, onehot], axis=0))
            for n, t in enumerate(group):
                other = [None] * 3
                for r in range(SLOTS // 8):
                    dx, dy, dz, falloff, decaying = geometry(c, t, 8 * r, 8)
                    q0, q1, q2, q3 = (
                        e * gathered[k * SLOTS + 8 * r : k * SLOTS + 8 * r + 8, n * 128 : (n + 1) * 128]
                        for k, e in enumerate(decaying)
                    )
                    plain = (q0 + q1) + (q2 + q3)
                    graded = q0 + 3.0 * (q1 + 3.0 * (q2 + 3.0 * q3))
                    pair = falloff * (falloff * graded + plain)
                    for q, delta in enumerate((dx, dy, dz)):
                        term = pair * delta
                        own[q][r] = term if own[q][r] is None else own[q][r] + term
                        other[q] = term if other[q] is None else other[q] + term
                for q in range(3):
                    racc[t, q] = racc[t, q] + other[q]
        for q in range(3):
            for r in range(SLOTS // 8):
                place = slice(q * SLOTS + 8 * r, q * SLOTS + 8 * r + 8)
                dacc[c, place, :] = own[q][r] if first else dacc[c, place, :] + own[q][r]

    def give_back(t, halves=(0, 1)):
        low = lax.broadcasted_iota(jnp.int32, (1, 128), 1) < SLOTS
        fx, fy, fz = (-FORCE_SCALE * jnp.sum(racc[t, q], axis=0, keepdims=True) for q in range(3))
        swap = lambda v: pltpu.roll(v, SLOTS, 1)
        for half in halves:
            r, x, y = PAIRS[t][half]
            if half:
                back[r, x, y, 0:1, :] = jnp.where(low, swap(fx), fy)
                back[r, x, y, 1:2, :] = jnp.where(low, swap(fz), 0.0)
            else:
                back[r, x, y, 0:1, :] = jnp.where(low, fx, swap(fy))
                back[r, x, y, 1:2, :] = jnp.where(low, fz, 0.0)

    def collect(n):
        role, dx, dy = DIRS[n]
        (xs, xe), (ys_, ye) = halo_part(dx), halo_part(dy)
        return pltpu.make_async_remote_copy(
            src_ref=back.at[role, xs:xe, ys_:ye],
            dst_ref=rec.at[n, 0 : xe - xs, 0 : ye - ys_],
            send_sem=send2.at[n],
            recv_sem=recv2.at[n],
            device_id=device(role, dx, dy),
            device_id_type=MESH,
        )

    racc[...] = jnp.zeros_like(racc)

    def arrive(wanted):
        for n, d in enumerate(DIRS):
            if wanted(d):
                out_copies[n].wait_recv()

    def take_in(wanted, first=False):
        for t, pair in enumerate(PAIRS):
            if wanted(pair):
                pair_tile(t, *pair)
        for c in range(4):
            part = weight_sums(c, tiles_of(c, wanted))
            sbuf[c] = part if first else sbuf[c] + part

    arrive(lambda d: d == (NEAR, 0, 0))
    take_in(is_own, True)
    arrive(lambda d: d[0] != FAR and d != (NEAR, 0, 0))
    take_in(is_side)
    arrive(lambda d: d == (FAR, 0, 0))
    take_in(is_far_core)
    arrive(lambda d: d[0] == FAR and d[1:] != (0, 0))
    take_in(is_far_ring)

    slot_row = lax.broadcasted_iota(jnp.int32, (SLOTS, CH), 0)
    split = []
    for c in range(4):
        sums = sbuf[c]
        wide = jnp.concatenate([sums[k * SLOTS : (k + 1) * SLOTS, :] for k in range(RAD)], axis=1)
        split += pieces(wide, 2)
    both = dot(jnp.concatenate(split, axis=0), table[...])
    message = jnp.concatenate(
        [both[c * 128 : c * 128 + 64, :] + both[c * 128 + 64 : c * 128 + 128, :] for c in range(4)], axis=0
    )
    message = (MSG_SCALE / HALF**4) * message
    sigmoid = 1.0 / (1.0 + jnp.exp(-message))
    act[...] = (message * sigmoid).astype(BF16).reshape(act.shape)
    occupied = jnp.concatenate([(slot_row < counts[c]).astype(F32) for c in range(4)], axis=0)
    adjoint = (occupied * sigmoid * (1.0 + message * (1.0 - sigmoid)) * rows[0:1, :]).astype(BF16)
    slopes = dot(adjoint, table[...], NT)
    for c in range(4):
        mine = slopes[c * SLOTS : (c + 1) * SLOTS, :]
        mine = jnp.concatenate([mine[:, k * SPEC : (k + 1) * SPEC] for k in range(RAD)], axis=0)
        abuf[c] = jnp.concatenate(pieces(mine, 2), axis=1)
    back_copies = [collect(n) for n in range(len(DIRS))]

    def send_back(wanted):
        for n, d in enumerate(DIRS):
            if wanted(d):
                back_copies[n].start()

    corners = [corner_of(c) for c in range(4)]
    for c in range(4):
        pair_forces(c, [corners[c][0]], True)
    for t, half in corners:
        give_back(t, (half,))
    send_back(lambda d: d[0] == FAR and 0 not in d[1:])

    def react(wanted):
        for c in range(4):
            pair_forces(c, [t for t in tiles_of(c, wanted) if t != corners[c][0]], False)
        for t, pair in enumerate(PAIRS):
            if wanted(pair):
                give_back(t, [h for h in (0, 1) if (t, h) not in corners])

    react(is_far_ring)
    send_back(lambda d: d[0] == FAR and d[1:].count(0) == 1)
    react(is_side)
    send_back(lambda d: d[0] != FAR and d[1:] != (0, 0))
    react(is_far_core)
    send_back(lambda d: d == (FAR, 0, 0))
    react(is_own)
    send_back(lambda d: d == (NEAR, 0, 0))

    occupied_rows = [(slot_lane < counts[c]).astype(F32) for c in range(4)]
    readout_rows = jnp.concatenate([p.astype(F32) for p in pieces(rows[0:1, :], 3)], axis=0).astype(BF16)
    species_rows = jnp.concatenate([p.astype(F32) for p in pieces(rows[1:2, :], 3)], axis=0).astype(BF16)
    for c in range(4):
        centre = hot[(1 + c // 2) * 4 + 1 + c % 2]
        parts = dot(readout_rows, act[c], NT) + dot(species_rows, centre)[:, 0:SLOTS]
        en_ref[c // 2, c % 2] = occupied_rows[c] * jnp.sum(parts, axis=0, keepdims=True)
    ones = jnp.ones((8, 128), F32)
    own = [FORCE_SCALE * dot(ones, dacc[c], NT, lax.Precision.HIGHEST)[0:1, :] for c in range(4)]
    for copy in back_copies:
        copy.wait_recv()
    for c in range(4):
        x, y = c // 2, c % 2
        total = back[CENTRE, 1 + x, 1 + y]
        for n, (role, dx, dy) in enumerate(DIRS):
            (xs, xe), (ys_, ye) = own_part(-dx), own_part(-dy)
            if xs <= x < xe and ys_ <= y < ye:
                total = total + rec[n, x - xs, y - ys_]
        planar = own[c][:, 0:128] + total[0:1, :]
        upright = own[c][:, 128:192] + total[1:2, 0:SLOTS]
        mask = occupied_rows[c]
        fo_ref[c // 2, c % 2, :, 0:128] = planar * jnp.concatenate([mask, mask], axis=1)
        fo_ref[c // 2, c % 2, :, 128:192] = upright * mask
    for copy in out_copies:
        copy.wait_send()
    for copy in back_copies:
        copy.wait_send()


def put_out(en_ref, fo_ref, en_out, fo_out, sems):
    copies = [pltpu.make_async_copy(en_ref, en_out, sems.at[0]), pltpu.make_async_copy(fo_ref, fo_out, sems.at[1])]
    for copy in copies:
        copy.start()
    for copy in copies:
        copy.wait()


def solution(mesh):
    sizes = tuple(mesh.shape[name] for name in ("gx", "gy", "gz"))
    in_specs = (
        P("gx", "gy", "gz", None),
        P("gx", "gy", "gz", None),
        P("gx", "gy", "gz"),
        P(),
        P(),
        P(),
        P(),
    )
    out_specs = (P("gx", "gy", "gz", None), P("gx", "gy", "gz", None))
    vmem = pl.BlockSpec(memory_space=pltpu.VMEM)
    anywhere = pl.BlockSpec(memory_space=pl.ANY)
    count = len(DIRS)

    def on_device(positions, species, counts, embed, filters, w_up, w_energy):
        operands = (
            positions,
            species,
            counts.transpose(0, 2, 1),
            embed,
            filters,
            w_up,
            w_energy.reshape(1, CH),
        )
        operands = [pltpu.with_memory_space_constraint(a, pltpu.HBM) for a in operands]
        results = pl.pallas_call(
            functools.partial(kernel, sizes),
            out_shape=(
                jax.ShapeDtypeStruct(species.shape, F32),
                jax.ShapeDtypeStruct(positions.shape, F32),
            ),
            in_specs=[anywhere] * len(operands),
            out_specs=(vmem, vmem),
            scratch_shapes=[pltpu.VMEM(a.shape, a.dtype) for a in operands]
            + [
                pltpu.SemaphoreType.DMA((len(operands),)),
                pltpu.VMEM((3, 4, 4, 2, 128), F32),
                pltpu.VMEM((count, 2, 2, 2, 128), F32),
                pltpu.VMEM((3, 4, 4, 2, 128), F32),
                pltpu.VMEM((24, 2, 128), F32),
                pltpu.VMEM((24, 2, 128), F32),
                pltpu.VMEM((24, SPEC, 128), BF16),
                pltpu.VMEM((4, 3, SLOTS, 128), F32),
                pltpu.VMEM((RAD * SPEC, CH), BF16),
                pltpu.VMEM((8, 128), F32),
                pltpu.VMEM((SPEC, CH), F32),
                pltpu.VMEM((4, RAD * SLOTS, SPEC), F32),
                pltpu.VMEM((4, RAD * SLOTS, 2 * SPEC), BF16),
                pltpu.VMEM((4, SLOTS, CH), BF16),
                pltpu.VMEM((24, 3, 8, 128), F32),
                pltpu.VMEM((4, 3 * SLOTS, 128), F32),
                pltpu.SemaphoreType.DMA((count,)),
                pltpu.SemaphoreType.DMA((count,)),
                pltpu.SemaphoreType.DMA((count,)),
                pltpu.SemaphoreType.DMA((count,)),
            ],
            compiler_params=pltpu.CompilerParams(
                collective_id=0, has_side_effects=True, vmem_limit_bytes=48 * 1024 * 1024
            ),
        )(*operands)
        return pl.pallas_call(
            put_out,
            out_shape=tuple(jax.ShapeDtypeStruct(a.shape, a.dtype) for a in results),
            in_specs=[anywhere] * 2,
            out_specs=(anywhere, anywhere),
            scratch_shapes=[pltpu.SemaphoreType.DMA((2,))],
            compiler_params=pltpu.CompilerParams(vmem_limit_bytes=1024 * 1024),
        )(*results)

    return jax.shard_map(
        on_device, mesh=mesh, in_specs=in_specs, out_specs=out_specs, check_vma=False
    )
```

```python
import functools

import jax
import jax.numpy as jnp
from jax import lax
from jax.experimental import pallas as pl
from jax.experimental.pallas import tpu as pltpu
from jax.sharding import PartitionSpec as P

MESH = pl.DeviceIdType.MESH
F32 = jnp.float32
BF16 = jnp.bfloat16

SLOTS = 64
CH = 128
RAD = 4
SPEC = 128
MSG_SCALE = 0.1
LOG2E = 1.4426950408889634
HALF = 0.5

FORCE_SCALE = -MSG_SCALE * 4 / HALF**3

CENTRE, NEAR, FAR = 0, 1, 2
NT = (((1,), (1,)), ((), ()))
NN = (((1,), (0,)), ((), ()))

DIRS = [
    (role, dx, dy)
    for role in (FAR, CENTRE, NEAR)
    for dx, dy in ((1, 1), (1, -1), (-1, 1), (-1, -1), (0, 1), (0, -1), (1, 0), (-1, 0), (0, 0))
    if (role, dx, dy) != (CENTRE, 0, 0)
]


def dot(a, b, dims=NN, precision=None):
    return lax.dot_general(a, b, dims, precision=precision, preferred_element_type=F32)


def pieces(values, count):
    out = []
    for _ in range(count):
        out.append(values.astype(BF16))
        values = values - out[-1].astype(F32)
    return out


def own_part(step):
    return {1: (1, 2), -1: (0, 1), 0: (0, 2)}[step]


def halo_part(step):
    return {1: (3, 4), -1: (0, 1), 0: (1, 3)}[step]


OWN_COLUMNS = [(x, y) for x in (1, 2) for y in (1, 2)]
PLANE_PAIRS = [((CENTRE, x, y), (NEAR, x, y)) for x in range(4) for y in range(4)]
FAR_PAIRS = [
    ((FAR,) + a, (FAR,) + b)
    for a, b in (
        ((0, 0), (3, 0)),
        ((0, 3), (3, 3)),
        ((1, 0), (2, 0)),
        ((1, 3), (2, 3)),
        ((0, 1), (0, 2)),
        ((3, 1), (3, 2)),
        ((1, 1), (1, 2)),
        ((2, 1), (2, 2)),
    )
]
PAIRS = PLANE_PAIRS + FAR_PAIRS


def tiles_of(c, wanted):
    x, y = 1 + c // 2, 1 + c % 2
    return [
        t
        for t, pair in enumerate(PAIRS)
        if wanted(pair) and any(abs(a - x) <= 1 and abs(b - y) <= 1 for _, a, b in pair)
    ]


def is_own(pair):
    return pair[0][0] != FAR and pair[0][1:] in OWN_COLUMNS


def is_side(pair):
    return pair[0][0] != FAR and pair[0][1:] not in OWN_COLUMNS


def is_far(pair):
    return pair[0][0] == FAR


def is_far_core(pair):
    return is_far(pair) and pair[0][1:] in OWN_COLUMNS


def is_far_corner(pair):
    return is_far(pair) and all(part in (0, 3) for part in pair[0][1:])


def is_far_side(pair):
    return is_far(pair) and not is_far_core(pair) and not is_far_corner(pair)


def rank(direction):
    role, dx, dy = direction
    if role == FAR:
        return 2 + abs(dx) + abs(dy)
    return 0 if direction == (NEAR, 0, 0) else 1


def cells_in(directions):
    return sum((2 - abs(dx)) * (2 - abs(dy)) for _, dx, dy in directions)


def kernel(
    sizes,
    pos_hbm,
    spec_hbm,
    cnt_hbm,
    embed_hbm,
    filt_hbm,
    wup_hbm,
    we_hbm,
    en_ref,
    fo_ref,
    pos_ref,
    spec_ref,
    cnt_ref,
    embed_ref,
    filt_ref,
    wup_ref,
    we_ref,
    fetch,
    pad,
    rec,
    back,
    xz,
    ys,
    hot,
    anchor,
    table,
    rows,
    emb,
    sbuf,
    abuf,
    act,
    racc,
    dacc,
    send1,
    recv1,
    send2,
    recv2,
):
    nx, ny, nz = sizes
    gx, gy, gz = (lax.axis_index(name) for name in ("gx", "gy", "gz"))
    odd = lax.rem(gz, 2)
    roles = (gz, gz + 1 - 2 * odd, lax.rem(gz + nz - 1 + 2 * odd, nz))

    def device(role, dx, dy):
        return (lax.rem(gx + nx + dx, nx), lax.rem(gy + ny + dy, ny), roles[role])

    operands = [
        (pos_hbm, pos_ref),
        (spec_hbm, spec_ref),
        (cnt_hbm, cnt_ref),
        (embed_hbm, embed_ref),
        (filt_hbm, filt_ref),
        (wup_hbm, wup_ref),
        (we_hbm, we_ref),
    ]
    loads = [pltpu.make_async_copy(a, b, fetch.at[n]) for n, (a, b) in enumerate(operands)]
    for load in loads[0:3]:
        load.start()
    barrier = pltpu.get_barrier_semaphore()
    for d in DIRS:
        pl.semaphore_signal(barrier, inc=1, device_id=device(*d), device_id_type=MESH)
    for load in loads[3:]:
        load.start()
    for load in loads[0:3]:
        load.wait()

    slot_lane = lax.broadcasted_iota(jnp.int32, (1, SLOTS), 1)
    counts = [cnt_ref[c // 2, 0:1, c % 2 : c % 2 + 1] for c in range(4)]
    places = [pos_ref.at[c // 2, c % 2] for c in range(4)]
    for c in range(4):
        marked = jnp.where(slot_lane < counts[c], spec_ref[c // 2, c % 2], -1).astype(F32)
        pad[CENTRE, 1 + c // 2, 1 + c % 2, 0:1, :] = places[c][:, 0:128]
        pad[CENTRE, 1 + c // 2, 1 + c % 2, 1:2, :] = jnp.concatenate(
            [places[c][:, 128:192], marked], axis=1
        )
    eye = lax.broadcasted_iota(jnp.int32, (SLOTS, SLOTS), 0) == lax.broadcasted_iota(
        jnp.int32, (SLOTS, SLOTS), 1
    )
    for c in range(4):
        for q in range(3):
            row = jnp.broadcast_to(places[c][:, q * SLOTS : (q + 1) * SLOTS], (SLOTS, SLOTS))
            column = jnp.sum(jnp.where(eye, row, 0.0), axis=1, keepdims=True)
            shift = (1.0 + c // 2, 1.0 + c % 2, 0.0)[q]
            anchor[c, q] = jnp.broadcast_to(HALF * (column + shift), (SLOTS, 128))
    for load in loads[3:]:
        load.wait()
    emb[...] = jnp.zeros_like(emb)
    emb[0 : embed_ref.shape[0], :] = embed_ref[...].astype(F32)
    embedding = emb[...].astype(BF16)
    for k in range(RAD):
        table[k * SPEC : (k + 1) * SPEC, :] = dot(
            embedding, filt_ref[:, k * CH : (k + 1) * CH]
        ).astype(BF16)
    energy_rows = jnp.concatenate([p.astype(F32) for p in pieces(we_ref[...], 3)], axis=0).astype(BF16)
    rows[0:1, :] = jnp.sum(dot(energy_rows, wup_ref[...], NT), axis=0, keepdims=True)
    rows[1:2, :] = jnp.sum(dot(energy_rows, embedding, NT), axis=0, keepdims=True)

    pl.semaphore_wait(barrier, len(DIRS))

    def spread(n):
        role, dx, dy = DIRS[n]
        (xs, xe), (ys_, ye) = own_part(dx), own_part(dy)
        (tx, te), (ty, tf) = halo_part(-dx), halo_part(-dy)
        return pltpu.make_async_remote_copy(
            src_ref=pad.at[CENTRE, 1 + xs : 1 + xe, 1 + ys_ : 1 + ye],
            dst_ref=pad.at[role, tx:te, ty:tf],
            send_sem=send1.at[0],
            recv_sem=recv1.at[rank(DIRS[n])],
            device_id=device(role, dx, dy),
            device_id_type=MESH,
        )

    out_copies = [spread(n) for n in range(len(DIRS))]
    for copy in out_copies:
        copy.start()

    lane2 = lax.broadcasted_iota(jnp.int32, (2, 128), 1)
    low2 = lane2 < SLOTS
    first2 = lax.broadcasted_iota(jnp.int32, (2, 128), 0) == 0
    species_row = lax.broadcasted_iota(jnp.int32, (SPEC, 128), 0).astype(F32)
    toward = (1 - 2 * odd).astype(F32)
    zoff = (jnp.zeros((), F32), toward, -toward)

    def pair_tile(t, cell_a, cell_b):
        (ra, xa, ya), (rb, xb, yb) = cell_a, cell_b
        a, b = pad[ra, xa, ya], pad[rb, xb, yb]
        a_swapped, b_swapped = pltpu.roll(a, SLOTS, 1), pltpu.roll(b, SLOTS, 1)
        offset = jnp.where(
            first2, jnp.where(low2, float(xa), float(xb)), jnp.where(low2, zoff[ra], zoff[rb])
        )
        xz[t] = HALF * (jnp.where(low2, a, b_swapped) + offset)
        mixed = jnp.where(low2, a_swapped, b)
        ys[t] = HALF * (mixed + jnp.where(first2, jnp.where(low2, float(ya), float(yb)), 0.0))
        hot[t] = jnp.where(species_row == mixed[1:2, :], 1.0, 0.0).astype(BF16)

    def geometry(c, t, lo, size):
        dx = xz[t, 0:1, :] - anchor[c, 0, lo : lo + size, :]
        dy = ys[t, 0:1, :] - anchor[c, 1, lo : lo + size, :]
        dz = xz[t, 1:2, :] - anchor[c, 2, lo : lo + size, :]
        dist_sq = dx * dx + dy * dy + dz * dz
        falloff = jnp.maximum(HALF * HALF - dist_sq, 0.0)
        decaying = [jnp.exp2((-0.5 * LOG2E * 3.0**k / HALF**2) * dist_sq) for k in range(RAD)]
        return dx, dy, dz, falloff, decaying

    def weight_sums(c, tiles):
        columns = []
        for t in tiles:
            blocks = [[] for _ in range(RAD)]
            for lo in range(0, SLOTS, 16):
                _, _, _, falloff, decaying = geometry(c, t, lo, 16)
                square = falloff * falloff
                if t == (1 + c // 2) * 4 + 1 + c % 2:
                    i = lax.broadcasted_iota(jnp.int32, (16, 128), 0) + lo
                    j = lax.broadcasted_iota(jnp.int32, (16, 128), 1)
                    square = jnp.where(i == j, 0.0, square)
                for k in range(RAD):
                    blocks[k].append((decaying[k] * square).astype(BF16))
            columns.append(jnp.concatenate(sum(blocks, []), axis=0))
        onehot = jnp.concatenate([hot[t] for t in tiles], axis=1)
        return dot(jnp.concatenate(columns, axis=1), onehot, NT)

    def pair_forces(c, tiles, first):
        own = [[None] * (SLOTS // 8) for _ in range(3)]
        for start in range(0, len(tiles), 2):
            group = tiles[start : start + 2]
            onehot = jnp.concatenate([hot[t] for t in group], axis=1)
            gathered = dot(abuf[c], jnp.concatenate([onehot, onehot], axis=0))
            for n, t in enumerate(group):
                other = [None] * 3
                for r in range(SLOTS // 8):
                    dx, dy, dz, falloff, decaying = geometry(c, t, 8 * r, 8)
                    q0, q1, q2, q3 = (
                        e * gathered[k * SLOTS + 8 * r : k * SLOTS + 8 * r + 8, n * 128 : (n + 1) * 128]
                        for k, e in enumerate(decaying)
                    )
                    plain = (q0 + q1) + (q2 + q3)
                    graded = q0 + 3.0 * (q1 + 3.0 * (q2 + 3.0 * q3))
                    pair = falloff * (falloff * graded + plain)
                    for q, delta in enumerate((dx, dy, dz)):
                        term = pair * delta
                        own[q][r] = term if own[q][r] is None else own[q][r] + term
                        other[q] = term if other[q] is None else other[q] + term
                for q in range(3):
                    racc[t, q] = racc[t, q] + other[q]
        for q in range(3):
            for r in range(SLOTS // 8):
                place = slice(q * SLOTS + 8 * r, q * SLOTS + 8 * r + 8)
                dacc[c, place, :] = own[q][r] if first else dacc[c, place, :] + own[q][r]

    def give_back(t):
        low = lax.broadcasted_iota(jnp.int32, (1, 128), 1) < SLOTS
        fx, fy, fz = (-FORCE_SCALE * jnp.sum(racc[t, q], axis=0, keepdims=True) for q in range(3))
        swap = lambda v: pltpu.roll(v, SLOTS, 1)
        (ra, xa, ya), (rb, xb, yb) = PAIRS[t]
        back[ra, xa, ya, 0:1, :] = jnp.where(low, fx, swap(fy))
        back[ra, xa, ya, 1:2, :] = jnp.where(low, fz, 0.0)
        back[rb, xb, yb, 0:1, :] = jnp.where(low, swap(fx), fy)
        back[rb, xb, yb, 1:2, :] = jnp.where(low, swap(fz), 0.0)

    def collect(n):
        role, dx, dy = DIRS[n]
        (xs, xe), (ys_, ye) = halo_part(dx), halo_part(dy)
        return pltpu.make_async_remote_copy(
            src_ref=back.at[role, xs:xe, ys_:ye],
            dst_ref=rec.at[n, 0 : xe - xs, 0 : ye - ys_],
            send_sem=send2.at[0],
            recv_sem=recv2.at[0],
            device_id=device(role, dx, dy),
            device_id_type=MESH,
        )

    racc[...] = jnp.zeros_like(racc)

    def finish(semaphore, directions):
        shape_of = rec.at[0 : cells_in(directions) // 4]
        pltpu.make_async_copy(shape_of, shape_of, semaphore).wait()

    def arrive(order):
        finish(recv1.at[order], [d for d in DIRS if rank(d) == order])

    def take_in(wanted, first=False):
        for t, pair in enumerate(PAIRS):
            if wanted(pair):
                pair_tile(t, *pair)
        for c in range(4):
            part = weight_sums(c, tiles_of(c, wanted))
            sbuf[c] = part if first else sbuf[c] + part

    arrive(0)
    take_in(is_own, True)
    arrive(1)
    take_in(is_side)
    arrive(2)
    take_in(is_far_core)
    arrive(3)
    take_in(is_far_side)
    arrive(4)
    take_in(is_far_corner)

    slot_row = lax.broadcasted_iota(jnp.int32, (SLOTS, CH), 0)
    split = []
    for c in range(4):
        sums = sbuf[c]
        wide = jnp.concatenate([sums[k * SLOTS : (k + 1) * SLOTS, :] for k in range(RAD)], axis=1)
        split += pieces(wide, 2)
    both = dot(jnp.concatenate(split, axis=0), table[...])
    message = jnp.concatenate(
        [both[c * 128 : c * 128 + 64, :] + both[c * 128 + 64 : c * 128 + 128, :] for c in range(4)], axis=0
    )
    message = (MSG_SCALE / HALF**4) * message
    sigmoid = 1.0 / (1.0 + jnp.exp(-message))
    act[...] = (message * sigmoid).astype(BF16).reshape(act.shape)
    occupied = jnp.concatenate([(slot_row < counts[c]).astype(F32) for c in range(4)], axis=0)
    adjoint = (occupied * sigmoid * (1.0 + message * (1.0 - sigmoid)) * rows[0:1, :]).astype(BF16)
    slopes = dot(adjoint, table[...], NT)
    for c in range(4):
        mine = slopes[c * SLOTS : (c + 1) * SLOTS, :]
        mine = jnp.concatenate([mine[:, k * SPEC : (k + 1) * SPEC] for k in range(RAD)], axis=0)
        abuf[c] = jnp.concatenate(pieces(mine, 2), axis=1)
    back_copies = [collect(n) for n in range(len(DIRS))]

    def react(wanted, sends, first=False):
        for c in range(4):
            pair_forces(c, tiles_of(c, wanted), first)
        for t, pair in enumerate(PAIRS):
            if wanted(pair):
                give_back(t)
        for n, d in enumerate(DIRS):
            if sends(d):
                back_copies[n].start()

    react(is_far_corner, lambda d: rank(d) == 4, True)
    react(is_far_side, lambda d: rank(d) == 3)
    react(is_side, lambda d: rank(d) == 1)
    react(is_far_core, lambda d: rank(d) == 2)
    react(is_own, lambda d: rank(d) == 0)

    occupied_rows = [(slot_lane < counts[c]).astype(F32) for c in range(4)]
    readout_rows = jnp.concatenate([p.astype(F32) for p in pieces(rows[0:1, :], 3)], axis=0).astype(BF16)
    species_rows = jnp.concatenate([p.astype(F32) for p in pieces(rows[1:2, :], 3)], axis=0).astype(BF16)
    for c in range(4):
        centre = hot[(1 + c // 2) * 4 + 1 + c % 2]
        parts = dot(readout_rows, act[c], NT) + dot(species_rows, centre)[:, 0:SLOTS]
        en_ref[c // 2, c % 2] = occupied_rows[c] * jnp.sum(parts, axis=0, keepdims=True)
    ones = jnp.ones((8, 128), F32)
    own = [FORCE_SCALE * dot(ones, dacc[c], NT, lax.Precision.HIGHEST)[0:1, :] for c in range(4)]
    finish(recv2.at[0], DIRS)
    for c in range(4):
        x, y = c // 2, c % 2
        total = back[CENTRE, 1 + x, 1 + y]
        for n, (role, dx, dy) in enumerate(DIRS):
            (xs, xe), (ys_, ye) = own_part(-dx), own_part(-dy)
            if xs <= x < xe and ys_ <= y < ye:
                total = total + rec[n, x - xs, y - ys_]
        planar = own[c][:, 0:128] + total[0:1, :]
        upright = own[c][:, 128:192] + total[1:2, 0:SLOTS]
        mask = occupied_rows[c]
        fo_ref[c // 2, c % 2, :, 0:128] = planar * jnp.concatenate([mask, mask], axis=1)
        fo_ref[c // 2, c % 2, :, 128:192] = upright * mask
    finish(send1.at[0], DIRS)
    finish(send2.at[0], DIRS)


def put_out(en_ref, fo_ref, en_out, fo_out, sems):
    copies = [pltpu.make_async_copy(en_ref, en_out, sems.at[0]), pltpu.make_async_copy(fo_ref, fo_out, sems.at[1])]
    for copy in copies:
        copy.start()
    for copy in copies:
        copy.wait()


def solution(mesh):
    sizes = tuple(mesh.shape[name] for name in ("gx", "gy", "gz"))
    in_specs = (
        P("gx", "gy", "gz", None),
        P("gx", "gy", "gz", None),
        P("gx", "gy", "gz"),
        P(),
        P(),
        P(),
        P(),
    )
    out_specs = (P("gx", "gy", "gz", None), P("gx", "gy", "gz", None))
    vmem = pl.BlockSpec(memory_space=pltpu.VMEM)
    anywhere = pl.BlockSpec(memory_space=pl.ANY)
    count = len(DIRS)

    def on_device(positions, species, counts, embed, filters, w_up, w_energy):
        operands = (
            positions,
            species,
            counts.transpose(0, 2, 1),
            embed,
            filters,
            w_up,
            w_energy.reshape(1, CH),
        )
        operands = [pltpu.with_memory_space_constraint(a, pltpu.HBM) for a in operands]
        results = pl.pallas_call(
            functools.partial(kernel, sizes),
            out_shape=(
                jax.ShapeDtypeStruct(species.shape, F32),
                jax.ShapeDtypeStruct(positions.shape, F32),
            ),
            in_specs=[anywhere] * len(operands),
            out_specs=(vmem, vmem),
            scratch_shapes=[pltpu.VMEM(a.shape, a.dtype) for a in operands]
            + [
                pltpu.SemaphoreType.DMA((len(operands),)),
                pltpu.VMEM((3, 4, 4, 2, 128), F32),
                pltpu.VMEM((count, 2, 2, 2, 128), F32),
                pltpu.VMEM((3, 4, 4, 2, 128), F32),
                pltpu.VMEM((24, 2, 128), F32),
                pltpu.VMEM((24, 2, 128), F32),
                pltpu.VMEM((24, SPEC, 128), BF16),
                pltpu.VMEM((4, 3, SLOTS, 128), F32),
                pltpu.VMEM((RAD * SPEC, CH), BF16),
                pltpu.VMEM((8, 128), F32),
                pltpu.VMEM((SPEC, CH), F32),
                pltpu.VMEM((4, RAD * SLOTS, SPEC), F32),
                pltpu.VMEM((4, RAD * SLOTS, 2 * SPEC), BF16),
                pltpu.VMEM((4, SLOTS, CH), BF16),
                pltpu.VMEM((24, 3, 8, 128), F32),
                pltpu.VMEM((4, 3 * SLOTS, 128), F32),
                pltpu.SemaphoreType.DMA((1,)),
                pltpu.SemaphoreType.DMA((5,)),
                pltpu.SemaphoreType.DMA((1,)),
                pltpu.SemaphoreType.DMA((1,)),
            ],
            compiler_params=pltpu.CompilerParams(
                collective_id=0, has_side_effects=True, vmem_limit_bytes=48 * 1024 * 1024
            ),
        )(*operands)
        return pl.pallas_call(
            put_out,
            out_shape=tuple(jax.ShapeDtypeStruct(a.shape, a.dtype) for a in results),
            in_specs=[anywhere] * 2,
            out_specs=(anywhere, anywhere),
            scratch_shapes=[pltpu.SemaphoreType.DMA((2,))],
            compiler_params=pltpu.CompilerParams(vmem_limit_bytes=1024 * 1024),
        )(*results)

    return jax.shard_map(
        on_device, mesh=mesh, in_specs=in_specs, out_specs=out_specs, check_vma=False
    )
```

```python
import functools

import jax
import jax.numpy as jnp
from jax import lax
from jax.experimental import pallas as pl
from jax.experimental.pallas import tpu as pltpu
from jax.sharding import PartitionSpec as P

MESH = pl.DeviceIdType.MESH
F32 = jnp.float32
BF16 = jnp.bfloat16

SLOTS = 64
CH = 128
RAD = 4
SPEC = 128
MSG_SCALE = 0.1
LOG2E = 1.4426950408889634
HALF = 0.5

FORCE_SCALE = -MSG_SCALE * 4 / HALF**3

CENTRE, NEAR, FAR = 0, 1, 2
NT = (((1,), (1,)), ((), ()))
NN = (((1,), (0,)), ((), ()))

DIRS = [
    (role, dx, dy)
    for role in (FAR, CENTRE, NEAR)
    for dx, dy in ((1, 1), (1, -1), (-1, 1), (-1, -1), (0, 1), (0, -1), (1, 0), (-1, 0), (0, 0))
    if (role, dx, dy) != (CENTRE, 0, 0)
]


def dot(a, b, dims=NN, precision=None):
    return lax.dot_general(a, b, dims, precision=precision, preferred_element_type=F32)


def pieces(values, count):
    out = []
    for _ in range(count):
        out.append(values.astype(BF16))
        values = values - out[-1].astype(F32)
    return out


def own_part(step):
    return {1: (1, 2), -1: (0, 1), 0: (0, 2)}[step]


def halo_part(step):
    return {1: (3, 4), -1: (0, 1), 0: (1, 3)}[step]


OWN_COLUMNS = [(x, y) for x in (1, 2) for y in (1, 2)]
PLANE_PAIRS = [((CENTRE, x, y), (NEAR, x, y)) for x in range(4) for y in range(4)]
FAR_PAIRS = [
    ((FAR,) + a, (FAR,) + b)
    for a, b in (
        ((0, 0), (3, 0)),
        ((0, 3), (3, 3)),
        ((1, 0), (2, 0)),
        ((1, 3), (2, 3)),
        ((0, 1), (0, 2)),
        ((3, 1), (3, 2)),
        ((1, 1), (1, 2)),
        ((2, 1), (2, 2)),
    )
]
PAIRS = PLANE_PAIRS + FAR_PAIRS


def tiles_of(c, wanted):
    x, y = 1 + c // 2, 1 + c % 2
    return [
        t
        for t, pair in enumerate(PAIRS)
        if wanted(pair) and any(abs(a - x) <= 1 and abs(b - y) <= 1 for _, a, b in pair)
    ]


def is_own(pair):
    return pair[0][0] != FAR and pair[0][1:] in OWN_COLUMNS


def is_side(pair):
    return pair[0][0] != FAR and pair[0][1:] not in OWN_COLUMNS


def is_far(pair):
    return pair[0][0] == FAR


def is_far_core(pair):
    return is_far(pair) and pair[0][1:] in OWN_COLUMNS


def is_far_corner(pair):
    return is_far(pair) and all(part in (0, 3) for part in pair[0][1:])


def is_far_side(pair):
    return is_far(pair) and not is_far_core(pair) and not is_far_corner(pair)


def rank(direction):
    role, dx, dy = direction
    if role == FAR:
        return 2 + abs(dx) + abs(dy)
    return 0 if direction == (NEAR, 0, 0) else 1


def cells_in(directions):
    return sum((2 - abs(dx)) * (2 - abs(dy)) for _, dx, dy in directions)


def kernel(
    sizes,
    pos_hbm,
    spec_hbm,
    cnt_hbm,
    embed_hbm,
    filt_hbm,
    wup_hbm,
    we_hbm,
    en_ref,
    fo_ref,
    pos_ref,
    spec_ref,
    cnt_ref,
    embed_ref,
    filt_ref,
    wup_ref,
    we_ref,
    fetch,
    pad,
    rec,
    back,
    xz,
    ys,
    hot,
    anchor,
    table,
    rows,
    emb,
    sbuf,
    abuf,
    act,
    racc,
    dacc,
    geo,
    send1,
    recv1,
    send2,
    recv2,
):
    nx, ny, nz = sizes
    gx, gy, gz = (lax.axis_index(name) for name in ("gx", "gy", "gz"))
    odd = lax.rem(gz, 2)
    roles = (gz, gz + 1 - 2 * odd, lax.rem(gz + nz - 1 + 2 * odd, nz))

    def device(role, dx, dy):
        return (lax.rem(gx + nx + dx, nx), lax.rem(gy + ny + dy, ny), roles[role])

    operands = [
        (pos_hbm, pos_ref),
        (spec_hbm, spec_ref),
        (cnt_hbm, cnt_ref),
        (embed_hbm, embed_ref),
        (filt_hbm, filt_ref),
        (wup_hbm, wup_ref),
        (we_hbm, we_ref),
    ]
    loads = [pltpu.make_async_copy(a, b, fetch.at[n]) for n, (a, b) in enumerate(operands)]
    for load in loads[0:3]:
        load.start()
    barrier = pltpu.get_barrier_semaphore()
    for d in DIRS:
        pl.semaphore_signal(barrier, inc=1, device_id=device(*d), device_id_type=MESH)
    for load in loads[3:]:
        load.start()
    for load in loads[0:3]:
        load.wait()

    slot_lane = lax.broadcasted_iota(jnp.int32, (1, SLOTS), 1)
    counts = [cnt_ref[c // 2, 0:1, c % 2 : c % 2 + 1] for c in range(4)]
    places = [pos_ref.at[c // 2, c % 2] for c in range(4)]
    for c in range(4):
        marked = jnp.where(slot_lane < counts[c], spec_ref[c // 2, c % 2], -1).astype(F32)
        pad[CENTRE, 1 + c // 2, 1 + c % 2, 0:1, :] = places[c][:, 0:128]
        pad[CENTRE, 1 + c // 2, 1 + c % 2, 1:2, :] = jnp.concatenate(
            [places[c][:, 128:192], marked], axis=1
        )
    eye = lax.broadcasted_iota(jnp.int32, (SLOTS, SLOTS), 0) == lax.broadcasted_iota(
        jnp.int32, (SLOTS, SLOTS), 1
    )
    for c in range(4):
        for q in range(3):
            row = jnp.broadcast_to(places[c][:, q * SLOTS : (q + 1) * SLOTS], (SLOTS, SLOTS))
            column = jnp.sum(jnp.where(eye, row, 0.0), axis=1, keepdims=True)
            shift = (1.0 + c // 2, 1.0 + c % 2, 0.0)[q]
            anchor[c, q] = jnp.broadcast_to(HALF * (column + shift), (SLOTS, 128))
    for load in loads[3:]:
        load.wait()
    emb[...] = jnp.zeros_like(emb)
    emb[0 : embed_ref.shape[0], :] = embed_ref[...].astype(F32)
    embedding = emb[...].astype(BF16)
    for k in range(RAD):
        table[k * SPEC : (k + 1) * SPEC, :] = dot(
            embedding, filt_ref[:, k * CH : (k + 1) * CH]
        ).astype(BF16)
    energy_rows = jnp.concatenate([p.astype(F32) for p in pieces(we_ref[...], 3)], axis=0).astype(BF16)
    rows[0:1, :] = jnp.sum(dot(energy_rows, wup_ref[...], NT), axis=0, keepdims=True)
    rows[1:2, :] = jnp.sum(dot(energy_rows, embedding, NT), axis=0, keepdims=True)

    pl.semaphore_wait(barrier, len(DIRS))

    def spread(n):
        role, dx, dy = DIRS[n]
        (xs, xe), (ys_, ye) = own_part(dx), own_part(dy)
        (tx, te), (ty, tf) = halo_part(-dx), halo_part(-dy)
        return pltpu.make_async_remote_copy(
            src_ref=pad.at[CENTRE, 1 + xs : 1 + xe, 1 + ys_ : 1 + ye],
            dst_ref=pad.at[role, tx:te, ty:tf],
            send_sem=send1.at[0],
            recv_sem=recv1.at[rank(DIRS[n])],
            device_id=device(role, dx, dy),
            device_id_type=MESH,
        )

    out_copies = [spread(n) for n in range(len(DIRS))]
    for copy in out_copies:
        copy.start()

    lane2 = lax.broadcasted_iota(jnp.int32, (2, 128), 1)
    low2 = lane2 < SLOTS
    first2 = lax.broadcasted_iota(jnp.int32, (2, 128), 0) == 0
    species_row = lax.broadcasted_iota(jnp.int32, (SPEC, 128), 0).astype(F32)
    toward = (1 - 2 * odd).astype(F32)
    zoff = (jnp.zeros((), F32), toward, -toward)

    def pair_tile(t, cell_a, cell_b):
        (ra, xa, ya), (rb, xb, yb) = cell_a, cell_b
        a, b = pad[ra, xa, ya], pad[rb, xb, yb]
        a_swapped, b_swapped = pltpu.roll(a, SLOTS, 1), pltpu.roll(b, SLOTS, 1)
        offset = jnp.where(
            first2, jnp.where(low2, float(xa), float(xb)), jnp.where(low2, zoff[ra], zoff[rb])
        )
        xz[t] = HALF * (jnp.where(low2, a, b_swapped) + offset)
        mixed = jnp.where(low2, a_swapped, b)
        ys[t] = HALF * (mixed + jnp.where(first2, jnp.where(low2, float(ya), float(yb)), 0.0))
        hot[t] = jnp.where(species_row == mixed[1:2, :], 1.0, 0.0).astype(BF16)

    def geometry(c, t, lo, size):
        dx = xz[t, 0:1, :] - anchor[c, 0, lo : lo + size, :]
        dy = ys[t, 0:1, :] - anchor[c, 1, lo : lo + size, :]
        dz = xz[t, 1:2, :] - anchor[c, 2, lo : lo + size, :]
        dist_sq = dx * dx + dy * dy + dz * dz
        falloff = jnp.maximum(HALF * HALF - dist_sq, 0.0)
        decaying = [jnp.exp2((-0.5 * LOG2E * 3.0**k / HALF**2) * dist_sq) for k in range(RAD)]
        return dx, dy, dz, falloff, decaying

    def keeps(t):
        return True

    def weight_sums(c, tiles):
        columns = []
        for t in tiles:
            blocks = [[] for _ in range(RAD)]
            for lo in range(0, SLOTS, 16):
                dx, dy, dz, falloff, decaying = geometry(c, t, lo, 16)
                if keeps(t):
                    for m, values in enumerate((dx, dy, dz, falloff, *decaying)):
                        geo[c, t, m, lo : lo + 16, :] = values
                square = falloff * falloff
                if t == (1 + c // 2) * 4 + 1 + c % 2:
                    i = lax.broadcasted_iota(jnp.int32, (16, 128), 0) + lo
                    j = lax.broadcasted_iota(jnp.int32, (16, 128), 1)
                    square = jnp.where(i == j, 0.0, square)
                for k in range(RAD):
                    blocks[k].append((decaying[k] * square).astype(BF16))
            columns.append(jnp.concatenate(sum(blocks, []), axis=0))
        onehot = jnp.concatenate([hot[t] for t in tiles], axis=1)
        return dot(jnp.concatenate(columns, axis=1), onehot, NT)

    def pair_forces(c, tiles, first):
        own = [[None] * (SLOTS // 8) for _ in range(3)]
        for start in range(0, len(tiles), 2):
            group = tiles[start : start + 2]
            onehot = jnp.concatenate([hot[t] for t in group], axis=1)
            gathered = dot(abuf[c], jnp.concatenate([onehot, onehot], axis=0))
            for n, t in enumerate(group):
                other = [None] * 3
                for r in range(SLOTS // 8):
                    if keeps(t):
                        dx, dy, dz, falloff, *decaying = (geo[c, t, m, 8 * r : 8 * r + 8, :] for m in range(8))
                    else:
                        dx, dy, dz, falloff, decaying = geometry(c, t, 8 * r, 8)
                    q0, q1, q2, q3 = (
                        e * gathered[k * SLOTS + 8 * r : k * SLOTS + 8 * r + 8, n * 128 : (n + 1) * 128]
                        for k, e in enumerate(decaying)
                    )
                    plain = (q0 + q1) + (q2 + q3)
                    graded = q0 + 3.0 * (q1 + 3.0 * (q2 + 3.0 * q3))
                    pair = falloff * (falloff * graded + plain)
                    for q, delta in enumerate((dx, dy, dz)):
                        term = pair * delta
                        own[q][r] = term if own[q][r] is None else own[q][r] + term
                        other[q] = term if other[q] is None else other[q] + term
                for q in range(3):
                    racc[t, q] = racc[t, q] + other[q]
        for q in range(3):
            for r in range(SLOTS // 8):
                place = slice(q * SLOTS + 8 * r, q * SLOTS + 8 * r + 8)
                dacc[c, place, :] = own[q][r] if first else dacc[c, place, :] + own[q][r]

    def give_back(t):
        low = lax.broadcasted_iota(jnp.int32, (1, 128), 1) < SLOTS
        fx, fy, fz = (-FORCE_SCALE * jnp.sum(racc[t, q], axis=0, keepdims=True) for q in range(3))
        swap = lambda v: pltpu.roll(v, SLOTS, 1)
        (ra, xa, ya), (rb, xb, yb) = PAIRS[t]
        back[ra, xa, ya, 0:1, :] = jnp.where(low, fx, swap(fy))
        back[ra, xa, ya, 1:2, :] = jnp.where(low, fz, 0.0)
        back[rb, xb, yb, 0:1, :] = jnp.where(low, swap(fx), fy)
        back[rb, xb, yb, 1:2, :] = jnp.where(low, swap(fz), 0.0)

    def collect(n):
        role, dx, dy = DIRS[n]
        (xs, xe), (ys_, ye) = halo_part(dx), halo_part(dy)
        return pltpu.make_async_remote_copy(
            src_ref=back.at[role, xs:xe, ys_:ye],
            dst_ref=rec.at[n, 0 : xe - xs, 0 : ye - ys_],
            send_sem=send2.at[0],
            recv_sem=recv2.at[0],
            device_id=device(role, dx, dy),
            device_id_type=MESH,
        )

    racc[...] = jnp.zeros_like(racc)

    def finish(semaphore, directions):
        shape_of = rec.at[0 : cells_in(directions) // 4]
        pltpu.make_async_copy(shape_of, shape_of, semaphore).wait()

    def arrive(order):
        finish(recv1.at[order], [d for d in DIRS if rank(d) == order])

    def take_in(wanted, first=False):
        for t, pair in enumerate(PAIRS):
            if wanted(pair):
                pair_tile(t, *pair)
        for c in range(4):
            part = weight_sums(c, tiles_of(c, wanted))
            sbuf[c] = part if first else sbuf[c] + part

    arrive(0)
    take_in(is_own, True)
    arrive(1)
    take_in(is_side)
    arrive(2)
    take_in(is_far_core)
    arrive(3)
    take_in(is_far_side)
    arrive(4)
    take_in(is_far_corner)

    slot_row = lax.broadcasted_iota(jnp.int32, (SLOTS, CH), 0)
    split = []
    for c in range(4):
        sums = sbuf[c]
        wide = jnp.concatenate([sums[k * SLOTS : (k + 1) * SLOTS, :] for k in range(RAD)], axis=1)
        split += pieces(wide, 2)
    both = dot(jnp.concatenate(split, axis=0), table[...])
    message = jnp.concatenate(
        [both[c * 128 : c * 128 + 64, :] + both[c * 128 + 64 : c * 128 + 128, :] for c in range(4)], axis=0
    )
    message = (MSG_SCALE / HALF**4) * message
    sigmoid = 1.0 / (1.0 + jnp.exp(-message))
    act[...] = (message * sigmoid).astype(BF16).reshape(act.shape)
    occupied = jnp.concatenate([(slot_row < counts[c]).astype(F32) for c in range(4)], axis=0)
    adjoint = (occupied * sigmoid * (1.0 + message * (1.0 - sigmoid)) * rows[0:1, :]).astype(BF16)
    slopes = dot(adjoint, table[...], NT)
    for c in range(4):
        mine = slopes[c * SLOTS : (c + 1) * SLOTS, :]
        mine = jnp.concatenate([mine[:, k * SPEC : (k + 1) * SPEC] for k in range(RAD)], axis=0)
        abuf[c] = jnp.concatenate(pieces(mine, 2), axis=1)
    back_copies = [collect(n) for n in range(len(DIRS))]

    def react(wanted, sends, first=False):
        for c in range(4):
            pair_forces(c, tiles_of(c, wanted), first)
        for t, pair in enumerate(PAIRS):
            if wanted(pair):
                give_back(t)
        for n, d in enumerate(DIRS):
            if sends(d):
                back_copies[n].start()

    react(is_far_corner, lambda d: rank(d) == 4, True)
    react(is_far_side, lambda d: rank(d) == 3)
    react(is_side, lambda d: rank(d) == 1)
    react(is_far_core, lambda d: rank(d) == 2)
    react(is_own, lambda d: rank(d) == 0)

    occupied_rows = [(slot_lane < counts[c]).astype(F32) for c in range(4)]
    readout_rows = jnp.concatenate([p.astype(F32) for p in pieces(rows[0:1, :], 3)], axis=0).astype(BF16)
    species_rows = jnp.concatenate([p.astype(F32) for p in pieces(rows[1:2, :], 3)], axis=0).astype(BF16)
    for c in range(4):
        centre = hot[(1 + c // 2) * 4 + 1 + c % 2]
        parts = dot(readout_rows, act[c], NT) + dot(species_rows, centre)[:, 0:SLOTS]
        en_ref[c // 2, c % 2] = occupied_rows[c] * jnp.sum(parts, axis=0, keepdims=True)
    ones = jnp.ones((8, 128), F32)
    own = [FORCE_SCALE * dot(ones, dacc[c], NT, lax.Precision.HIGHEST)[0:1, :] for c in range(4)]
    finish(recv2.at[0], DIRS)
    for c in range(4):
        x, y = c // 2, c % 2
        total = back[CENTRE, 1 + x, 1 + y]
        for n, (role, dx, dy) in enumerate(DIRS):
            (xs, xe), (ys_, ye) = own_part(-dx), own_part(-dy)
            if xs <= x < xe and ys_ <= y < ye:
                total = total + rec[n, x - xs, y - ys_]
        planar = own[c][:, 0:128] + total[0:1, :]
        upright = own[c][:, 128:192] + total[1:2, 0:SLOTS]
        mask = occupied_rows[c]
        fo_ref[c // 2, c % 2, :, 0:128] = planar * jnp.concatenate([mask, mask], axis=1)
        fo_ref[c // 2, c % 2, :, 128:192] = upright * mask
    finish(send1.at[0], DIRS)
    finish(send2.at[0], DIRS)


def put_out(en_ref, fo_ref, en_out, fo_out, sems):
    copies = [pltpu.make_async_copy(en_ref, en_out, sems.at[0]), pltpu.make_async_copy(fo_ref, fo_out, sems.at[1])]
    for copy in copies:
        copy.start()
    for copy in copies:
        copy.wait()


def solution(mesh):
    sizes = tuple(mesh.shape[name] for name in ("gx", "gy", "gz"))
    in_specs = (
        P("gx", "gy", "gz", None),
        P("gx", "gy", "gz", None),
        P("gx", "gy", "gz"),
        P(),
        P(),
        P(),
        P(),
    )
    out_specs = (P("gx", "gy", "gz", None), P("gx", "gy", "gz", None))
    vmem = pl.BlockSpec(memory_space=pltpu.VMEM)
    anywhere = pl.BlockSpec(memory_space=pl.ANY)
    count = len(DIRS)

    def on_device(positions, species, counts, embed, filters, w_up, w_energy):
        operands = (
            positions,
            species,
            counts.transpose(0, 2, 1),
            embed,
            filters,
            w_up,
            w_energy.reshape(1, CH),
        )
        operands = [pltpu.with_memory_space_constraint(a, pltpu.HBM) for a in operands]
        results = pl.pallas_call(
            functools.partial(kernel, sizes),
            out_shape=(
                jax.ShapeDtypeStruct(species.shape, F32),
                jax.ShapeDtypeStruct(positions.shape, F32),
            ),
            in_specs=[anywhere] * len(operands),
            out_specs=(vmem, vmem),
            scratch_shapes=[pltpu.VMEM(a.shape, a.dtype) for a in operands]
            + [
                pltpu.SemaphoreType.DMA((len(operands),)),
                pltpu.VMEM((3, 4, 4, 2, 128), F32),
                pltpu.VMEM((count, 2, 2, 2, 128), F32),
                pltpu.VMEM((3, 4, 4, 2, 128), F32),
                pltpu.VMEM((24, 2, 128), F32),
                pltpu.VMEM((24, 2, 128), F32),
                pltpu.VMEM((24, SPEC, 128), BF16),
                pltpu.VMEM((4, 3, SLOTS, 128), F32),
                pltpu.VMEM((RAD * SPEC, CH), BF16),
                pltpu.VMEM((8, 128), F32),
                pltpu.VMEM((SPEC, CH), F32),
                pltpu.VMEM((4, RAD * SLOTS, SPEC), F32),
                pltpu.VMEM((4, RAD * SLOTS, 2 * SPEC), BF16),
                pltpu.VMEM((4, SLOTS, CH), BF16),
                pltpu.VMEM((24, 3, 8, 128), F32),
                pltpu.VMEM((4, 3 * SLOTS, 128), F32),
                pltpu.VMEM((4, len(PAIRS), 8, SLOTS, 128), F32),
                pltpu.SemaphoreType.DMA((1,)),
                pltpu.SemaphoreType.DMA((5,)),
                pltpu.SemaphoreType.DMA((1,)),
                pltpu.SemaphoreType.DMA((1,)),
            ],
            compiler_params=pltpu.CompilerParams(
                collective_id=0, has_side_effects=True, vmem_limit_bytes=48 * 1024 * 1024
            ),
        )(*operands)
        return pl.pallas_call(
            put_out,
            out_shape=tuple(jax.ShapeDtypeStruct(a.shape, a.dtype) for a in results),
            in_specs=[anywhere] * 2,
            out_specs=(anywhere, anywhere),
            scratch_shapes=[pltpu.SemaphoreType.DMA((2,))],
            compiler_params=pltpu.CompilerParams(vmem_limit_bytes=1024 * 1024),
        )(*results)

    return jax.shard_map(
        on_device, mesh=mesh, in_specs=in_specs, out_specs=out_specs, check_vma=False
    )
```
